32 devices in a mesh: groups: 2 (over y), seq: 4 (over z), mp: 2 (over x), rep: 2 (over core).
Axes of the slice: x: 2, y: 2, z: 4, core: 2. Of those that a mesh axis runs over, the one named last changes fastest.
Arguments:
- queries: bfloat16 [2048, 2048], P(('groups', 'seq'), ('mp', 'rep')), parts along dimension 0, may hold values from -14 to 14
- keys: bfloat16 [2048, 2048], P(('groups', 'seq'), ('mp', 'rep')), parts along dimension 0, may hold values from -22 to 22
- values: bfloat16 [2048, 2048], P(('groups', 'seq'), ('mp', 'rep')), parts along dimension 0, may hold values from -40 to 40
- resid: bfloat16 [2048, 2048], P(('groups', 'seq'), ('mp', 'rep')), parts along dimension 0, may hold values from -6 to 6
- w_in: bfloat16 [8, 2048, 2048], P(('seq', 'rep'), None, 'mp'), may hold values from -0.125 to 0.125
- w_out: bfloat16 [8, 2048, 2048], P(('seq', 'rep'), 'mp'), may hold values from -0.125 to 0.125
- routes: int32 [2048, 2], P(('groups', 'seq')), parts along dimension 0, may hold values from 0 to 7, as said below
- gate_num: int32 [2048, 2], P(('groups', 'seq')), parts along dimension 0, may hold values from 200 to 256
Outputs:
- layer_out: bfloat16 [2048, 2048], P(('groups', 'seq'), ('mp', 'rep')), parts along dimension 0
The draws below stay inside these ranges and needn't reach their ends.
There are 2 independent parts, one for each index of `groups`. The reference program is written for one: setup_inputs(seed, part) draws one part's arguments, and reference() takes and returns one part's arrays. A program takes and returns all parts, laid end to end along the dimension named above; an argument that names none is the same for every part. Nothing has to cross between parts.
Inputs may be any that keep to these rules, and one draw needn't show every extreme that they name: `routes`: the two experts of an event differ. In each block of 256 consecutive events no expert is named more than 128 times, and one expert is named exactly 128 times in every block.
All inputs are finite; a program needn't handle non-finite values.
Results may differ from the reference program's by a relative error of at most 0.0095.
Values may be sent and summed in bfloat16 or wider, within the bound.
No kernel may reach another device: no remote copies, remote signals or barrier semaphores. Data moves between devices by JAX's collectives and lax.ppermute only.
A program may use at most 64 MiB of HBM per device.

```python
import jax
import jax.numpy as jnp
from jax import lax

D = 2048
H = 16
HD = 128
FF = 2048
TOP = 2
TOK = 256
E = 8
CAP = 128
TOKENS = 1024
FF_DEV = 1024
N_SEQ = 4
N_MP = 2


def base_field(key_base):
    return jnp.clip(jax.random.normal(key_base, (TOKENS, D), jnp.float32), -4.0, 4.0)


def draw_queries(key, part):
    key_base, key_scale = jax.random.split(jax.random.fold_in(key, 31), 2)
    base_draw = base_field(key_base).reshape(TOKENS, H, HD)
    head_scale = jnp.exp(jax.random.uniform(key_scale, (TOKENS, H, 1), jnp.float32, -1.2, 1.2))
    return (base_draw * head_scale).reshape(TOKENS, D).astype(jnp.bfloat16)


def draw_keys(key, part):
    key_base, key_block, key_event = jax.random.split(jax.random.fold_in(key, 43), 3)
    base_draw = base_field(key_base).reshape(TOKENS // TOK, TOK, H, HD)
    block_scale = jnp.exp(jax.random.uniform(key_block, (TOKENS // TOK, 1, H, 1), jnp.float32, -1.2, 1.2))
    event_scale = jnp.exp(jax.random.uniform(key_event, (TOKENS // TOK, TOK, H, 1), jnp.float32, -0.5, 0.5))
    return (base_draw * block_scale * event_scale).reshape(TOKENS, D).astype(jnp.bfloat16)


def draw_values(key, part):
    key_col, key_row, key_base = jax.random.split(key, 3)
    ramp = jnp.exp(jnp.arange(D, dtype=jnp.float32) * (1.098612 / (D - 1)))
    column_scale = jnp.exp(jax.random.uniform(key_col, (D,), jnp.float32, 0.0, 1.2)) * ramp
    row_scale = jnp.exp(jax.random.uniform(key_row, (TOKENS, 1), jnp.float32, 0.0, 1.386294))
    base_draw = jnp.clip(jax.random.normal(key_base, (TOKENS, D), jnp.float32), -3.9, 3.9)
    return (base_draw * column_scale[None, :] * row_scale * 0.25).astype(jnp.bfloat16)


def route_block(block_key, hot_expert):
    key_weight, key_score, key_swap, key_side, key_shuffle = jax.random.split(block_key, 5)
    other_experts = (hot_expert + 1 + jnp.arange(E - 1, dtype=jnp.int32)) % E
    slot_pool = jnp.repeat(other_experts, CAP, total_repeat_length=(E - 1) * CAP)
    pool_length = (E - 1) * CAP
    expert_weight = jnp.repeat(jax.random.randint(key_weight, (E - 1,), 1, 9, dtype=jnp.int32), CAP, total_repeat_length=pool_length)
    scores = jax.random.randint(key_score, (pool_length,), 0, 4096, dtype=jnp.int32) * expert_weight * pool_length
    scores = scores + jnp.arange(pool_length, dtype=jnp.int32)
    _, chosen_index = lax.top_k(scores, 2 * TOK - CAP)
    chosen = slot_pool[chosen_index]
    ordering = jnp.argsort(chosen, stable=True)
    ranked = chosen[ordering]
    pair_count = TOK - CAP
    first_pick = ranked[:pair_count]
    second = ranked[pair_count:2 * pair_count]
    hot_partner = ranked[2 * pair_count:]
    swap_bits = jax.random.randint(key_swap, (pair_count,), 0, 2, dtype=jnp.int32) == 1
    pair_rows = jnp.stack([jnp.where(swap_bits, second, first_pick), jnp.where(swap_bits, first_pick, second)], axis=1)
    side_bits = jax.random.randint(key_side, (CAP,), 0, 2, dtype=jnp.int32) == 1
    hot_column = jnp.full((CAP,), 0, jnp.int32) + hot_expert
    hot_rows = jnp.stack([jnp.where(side_bits, hot_partner, hot_column), jnp.where(side_bits, hot_column, hot_partner)], axis=1)
    all_rows = jnp.concatenate([pair_rows, hot_rows], axis=0)
    shuffle = jax.random.permutation(key_shuffle, TOK)
    return all_rows[shuffle]


def draw_routes(key, part):
    key_hot, key_blocks = jax.random.split(jax.random.fold_in(key, 17), 2)
    hot_expert = jax.random.randint(key_hot, (), 0, E, dtype=jnp.int32)
    block_keys = jax.random.split(key_blocks, TOKENS // TOK)
    blocks = jax.vmap(route_block, in_axes=(0, None))(block_keys, hot_expert)
    return blocks.reshape(TOKENS, TOP).astype(jnp.int32)


def set_ends(drawn, key, least, top_value):
    spot = [jax.random.randint(jax.random.fold_in(key, axis), (), 0, length) for axis, length in enumerate(drawn.shape)]
    widest = drawn.shape.index(max(drawn.shape))
    next_to = spot[:widest] + [(spot[widest] + 1) % drawn.shape[widest]] + spot[widest + 1:]
    return drawn.at[tuple(spot)].set(least).at[tuple(next_to)].set(top_value)


def shard_levels(stream_key, shape, cuts, low, top_value):
    gain = 1.0
    for axis_at, shards_of in cuts:
        draws = jax.random.uniform(jax.random.fold_in(jax.random.fold_in(stream_key, 6), axis_at), (shards_of,), jnp.float32, low / len(cuts), top_value / len(cuts))
        gain = gain * jnp.repeat(jnp.exp(draws), shape[axis_at] // shards_of).reshape((-1,) + (1,) * (len(shape) - 1 - axis_at))
    return gain


def centred(rng, extent, scale, limit, shards=(), kind=jnp.bfloat16):
    result = scale * jax.random.normal(rng, extent, jnp.float32)
    if shards:
        result = result * shard_levels(rng, extent, shards, -0.22, 0.18)
    return jnp.clip(result, -limit, limit).astype(kind)


def setup_inputs(seed: int = 0, part: int = 0) -> dict:
    splits = jax.random.split(jax.random.key(seed), 9)
    part_splits = jax.random.split(jax.random.fold_in(splits[8], part), 9)
    return {
        "queries": draw_queries(jax.random.fold_in(jax.random.fold_in(splits[8], part), 71), part),
        "keys": draw_keys(jax.random.fold_in(jax.random.fold_in(splits[8], part), 71), part),
        "values": draw_values(jax.random.fold_in(jax.random.fold_in(splits[8], part), 71), part),
        "resid": centred(part_splits[3], (TOKENS, D), 1.0, 6.0, ((0, 4), (1, 4))),
        "w_in": centred(splits[4], (E, D, FF), D ** -0.5, 0.125, ((0, 8), (2, 2))),
        "w_out": centred(splits[5], (E, FF, D), FF ** -0.5, 0.125, ((0, 8), (1, 2))),
        "routes": draw_routes(jax.random.fold_in(jax.random.fold_in(splits[8], part), 71), part),
        "gate_num": set_ends(jax.random.randint(part_splits[7], (TOKENS, TOP), 200, 257), jax.random.fold_in(part_splits[7], 1), 200, 256).astype(jnp.int32),
    }


gate_scale = 1.0 / 256.0
highest = lax.Precision.HIGHEST

def feature(inputs_raw):
    return jax.nn.elu(inputs_raw.astype(jnp.float32)) + 1.0

def block_step(carried, inputs):
    memory, key_total = carried
    block_query, block_key, block_value = inputs
    width = block_query.shape[1]
    causal = jnp.tril(jnp.ones((width, width), jnp.float32))
    scores = jnp.einsum('htc,hsc->hts', block_query, block_key, precision=highest) * causal
    numerator = jnp.einsum('hts,hsd->htd', scores, block_value, precision=highest)
    numerator = numerator + jnp.einsum('htc,hcd->htd', block_query, memory, precision=highest)
    denominator = lax.optimization_barrier(jnp.sum(scores, axis=-1)) + jnp.einsum('htc,hc->ht', block_query, key_total, precision=highest)
    attended = numerator / denominator[..., None]
    memory_next = memory + jnp.einsum('hsc,hsd->hcd', block_key, block_value, precision=highest)
    key_next = key_total + lax.optimization_barrier(jnp.sum(block_key, axis=1))
    return ((memory_next, key_next), attended)

def reference(queries, keys, values, resid, w_in, w_out, routes, gate_num):
    query_feat = feature(queries).reshape(N_SEQ, TOK, H, HD).transpose(0, 2, 1, 3)
    key_feat = feature(keys).reshape(N_SEQ, TOK, H, HD).transpose(0, 2, 1, 3)
    value_heads = values.astype(jnp.float32).reshape(N_SEQ, TOK, H, HD).transpose(0, 2, 1, 3)
    initial = (jnp.zeros((H, HD, HD), jnp.float32), jnp.zeros((H, HD), jnp.float32))
    _, attended = lax.scan(block_step, initial, (query_feat, key_feat, value_heads))
    row_mean = lax.optimization_barrier(jnp.mean(attended * attended, axis=(1, 3), keepdims=True))
    normed = attended * lax.rsqrt(row_mean + 1e-06)
    mixed_rows = (resid.astype(jnp.float32) + normed.transpose(0, 2, 1, 3).reshape(TOKENS, D)).astype(jnp.bfloat16)
    routed = routes.reshape(N_SEQ, TOK * TOP)
    onehot = (routed[:, :, None] == jnp.arange(E, dtype=jnp.int32)[None, None, :]).astype(jnp.int32)
    slot_rank = lax.optimization_barrier(jnp.sum((jnp.cumsum(onehot, axis=1) - onehot) * onehot, axis=2))
    slot_place = jnp.arange(N_SEQ, dtype=jnp.int32)[:, None] * CAP + slot_rank
    token_of = (jnp.arange(TOKENS * TOP, dtype=jnp.int32) // TOP).reshape(N_SEQ, TOK * TOP)
    slot_table = jnp.full((E, N_SEQ * CAP), TOKENS, jnp.int32).at[routed, slot_place].set(token_of)
    padded = jnp.concatenate([mixed_rows, jnp.zeros((1, D), jnp.bfloat16)], axis=0)

    def expert_apply(expert_id):
        expert_rows = padded[slot_table[expert_id]]
        preact = jnp.dot(expert_rows, w_in[expert_id], preferred_element_type=jnp.float32)
        hidden = jax.nn.gelu(preact).astype(jnp.bfloat16)
        blocks = jnp.einsum('rmf,mfd->mrd', hidden.reshape(-1, N_MP, FF_DEV).astype(jnp.float32), w_out[expert_id].reshape(N_MP, FF_DEV, D).astype(jnp.float32), precision=highest)
        rounded = lax.optimization_barrier(blocks.astype(jnp.bfloat16))
        return lax.optimization_barrier(jnp.sum(rounded.astype(jnp.float32), axis=0))
    results = lax.map(expert_apply, jnp.arange(E, dtype=jnp.int32))
    picked = results[routed, slot_place].reshape(TOKENS, TOP, D)
    gates = gate_num.astype(jnp.float32) * gate_scale
    summed = mixed_rows.astype(jnp.float32) + lax.optimization_barrier(jnp.sum(gates[:, :, None] * picked, axis=1))
    return summed.astype(jnp.bfloat16)
```

```python
import functools

import jax
import jax.numpy as jnp
from jax import lax
from jax.experimental import pallas as pl
from jax.experimental.pallas import tpu as pltpu
from jax.sharding import PartitionSpec as P

D = 2048
HD = 128
TOP = 2

gate_scale = 1.0 / 256.0
highest = lax.Precision.HIGHEST
f32 = jnp.float32
bf16 = jnp.bfloat16
VMEM = pl.BlockSpec(memory_space=pltpu.VMEM)
SMEM = pl.BlockSpec(memory_space=pltpu.SMEM)
LIMIT = pltpu.CompilerParams(vmem_limit_bytes=40 * 1024 * 1024)


def feature(inputs_raw):
    wide = inputs_raw.astype(f32)
    return jnp.where(wide > 0.0, wide + 1.0, jnp.exp(jnp.minimum(wide, 0.0)))


def heads_first(matrix, head_width):
    return matrix.reshape(matrix.shape[0], -1, head_width).transpose(1, 0, 2)


def general(queries, keys, values, resid, w_in, w_out, routes, gate_num):
    tok_count, col_count = queries.shape
    seq_count = lax.axis_size("seq")
    rep_count = lax.axis_size("rep")
    expert_count = seq_count * rep_count
    capacity = 2 * TOP * tok_count // expert_count
    slot_count = expert_count * capacity
    query_feat = heads_first(feature(queries), HD)
    key_feat = heads_first(feature(keys), HD)
    value_heads = heads_first(values.astype(f32), HD)
    memory = jnp.einsum("hsc,hsd->hcd", key_feat, value_heads, precision=highest)
    key_total = jnp.sum(key_feat, axis=1)
    state = jnp.concatenate([memory, key_total[:, None, :]], axis=1).astype(bf16)
    states = lax.all_gather(state, "seq").astype(f32)
    earlier = jnp.arange(seq_count) < lax.axis_index("seq")
    state = jnp.sum(jnp.where(earlier[:, None, None, None], states, 0.0), axis=0)
    before, before_total = state[:, :HD], state[:, HD]
    causal = jnp.tril(jnp.ones((tok_count, tok_count), f32))
    scores = jnp.einsum("htc,hsc->hts", query_feat, key_feat, precision=highest) * causal
    numerator = jnp.einsum("hts,hsd->htd", scores, value_heads, precision=highest)
    numerator = numerator + jnp.einsum("htc,hcd->htd", query_feat, before, precision=highest)
    denominator = jnp.sum(scores, axis=-1) + jnp.einsum(
        "htc,hc->ht", query_feat, before_total, precision=highest
    )
    attended = numerator / denominator[..., None]
    local_squares = jnp.sum(attended * attended, axis=(0, 2))
    row_squares = lax.psum(local_squares, ("mp", "rep"))
    normed = attended * lax.rsqrt(row_squares / D + 1e-06)[None, :, None]
    mixed_rows = (
        resid.astype(f32) + normed.transpose(1, 0, 2).reshape(tok_count, col_count)
    ).astype(bf16)
    routed = routes.reshape(-1)
    onehot = (routed[:, None] == jnp.arange(expert_count, dtype=jnp.int32)[None, :]).astype(f32)
    pairs = jnp.arange(tok_count * TOP)
    below = (pairs[:, None] > pairs[None, :]).astype(f32)
    counts = jnp.dot(below, onehot, precision=highest)
    slot_rank = jnp.sum(counts * onehot, axis=1).astype(jnp.int32)
    slot_index = (routed // rep_count * capacity + slot_rank) * rep_count + routed % rep_count
    matches = (slot_index[:, None] == jnp.arange(slot_count, dtype=jnp.int32)[None, :]).astype(f32)
    matches = matches.reshape(tok_count, TOP, slot_count)
    picker = jnp.sum(matches, axis=1).astype(bf16)
    weights = gate_num.astype(f32) * gate_scale
    combine = jnp.einsum("tk,tks->ts", weights, matches, precision=highest)
    outgoing = jnp.einsum("ts,tc->sc", picker, mixed_rows, preferred_element_type=f32).astype(bf16)

    def exchange(rows):
        rows = rows.reshape(seq_count, capacity, rep_count, col_count)
        rows = lax.all_to_all(rows, "seq", split_axis=0, concat_axis=0, tiled=True)
        return lax.all_to_all(rows, "rep", split_axis=2, concat_axis=2, tiled=True)

    expert_rows = exchange(outgoing).reshape(seq_count * capacity, rep_count * col_count)
    preact = jnp.dot(
        lax.all_gather(expert_rows, "mp", axis=1, tiled=True), w_in[0], preferred_element_type=f32
    )
    hidden = jax.nn.gelu(preact).astype(bf16)
    partial_value = jnp.dot(hidden, w_out[0], preferred_element_type=f32)
    summed = lax.psum_scatter(partial_value.astype(bf16), "mp", scatter_dimension=1, tiled=True)
    returned = exchange(summed).astype(f32)
    expert_mix = jnp.dot(combine, returned.reshape(slot_count, col_count), precision=highest)
    return (mixed_rows.astype(f32) + expert_mix).astype(bf16)


def nt(a, b):
    return lax.dot_general(a, b, (((1,), (1,)), ((), ())), preferred_element_type=f32)


def tn(a, b):
    return lax.dot_general(a, b, (((0,), (0,)), ((), ())), preferred_element_type=f32)


def state_kernel(heads, k_ref, v_ref, state_ref):
    totals = []
    for h in range(heads):
        cols = pl.ds(h * HD, HD)
        key = feature(k_ref[:, cols])
        state_ref[pl.ds(h * HD, HD), :] = tn(v_ref[:, cols], key.astype(bf16)).astype(bf16)
        totals.append(jnp.sum(key, axis=0, keepdims=True))
    totals.append(jnp.zeros((16 - heads, HD), f32))
    state_ref[pl.ds(heads * HD, 16), :] = jnp.concatenate(totals, axis=0).astype(bf16)


def local_kernel(heads, q_ref, k_ref, v_ref, num_ref, den_ref):
    rows = q_ref.shape[0]
    t = lax.broadcasted_iota(jnp.int32, (rows, rows), 0)
    s = lax.broadcasted_iota(jnp.int32, (rows, rows), 1)
    for h in range(heads):
        cols = pl.ds(h * HD, HD)
        query = feature(q_ref[:, cols]).astype(bf16)
        key = feature(k_ref[:, cols]).astype(bf16)
        scores = jnp.where(s <= t, nt(query, key), 0.0).astype(bf16)
        num_ref[:, cols] = jnp.dot(scores, v_ref[:, cols], preferred_element_type=f32)
        den_ref[:, cols] = jnp.dot(scores, jnp.ones((rows, HD), bf16), preferred_element_type=f32)


def carry_kernel(heads, n, q_ref, num_ref, den_ref, *refs):
    states, (att_ref, sq_ref) = refs[:n], refs[n:]
    rows = q_ref.shape[0]
    squares = jnp.zeros((rows, HD), f32)
    carried = states[0][...].astype(f32)
    for extra in states[1:]:
        carried = carried + extra[...].astype(f32)
    carried = carried.astype(bf16)
    for h in range(heads):
        cols = pl.ds(h * HD, HD)
        query = feature(q_ref[:, cols]).astype(bf16)
        top = num_ref[:, cols] + nt(query, carried[h * HD : (h + 1) * HD])
        total = jnp.broadcast_to(carried[heads * HD + h : heads * HD + h + 1], (HD, HD))
        attended = top / (den_ref[:, cols] + nt(query, total))
        att_ref[:, cols] = attended
        squares = squares + attended * attended
    summed = lax.dot_general(
        jnp.ones((8, HD), f32), squares, (((1,), (1,)), ((), ())),
        preferred_element_type=f32, precision=highest,
    )
    sq_ref[...] = summed


def mix_kernel(n, resid_ref, att_ref, *refs):
    squares, mixed_ref = refs[:n], refs[n]
    total = squares[0][...]
    for extra in squares[1:]:
        total = total + extra[...]
    scale = lax.rsqrt(total * (1.0 / D) + 1e-06)
    column = jnp.transpose(scale)[:, :1]
    mixed_ref[...] = (resid_ref[...].astype(f32) + att_ref[...] * column).astype(bf16)


def route_kernel(n, idx_ref, *refs):
    blocks, out_ref = refs[:n], refs[n]
    expert = idx_ref[0]
    width = out_ref.shape[2]
    a = lax.broadcasted_iota(jnp.int32, (width, width), 0)
    b = lax.broadcasted_iota(jnp.int32, (width, width), 1)
    before = jnp.where(a < b, 1.0, 0.0).astype(bf16)
    for k in range(n):
        block = blocks[k][...]
        first = block[0:1] == expert
        second = block[1:2] == expert
        named = first | second
        flag = jnp.broadcast_to(jnp.where(named, 1.0, 0.0), (8, width)).astype(bf16)
        rank = jnp.dot(flag, before, preferred_element_type=f32)
        slot = jnp.where(named, rank[0:1], -1.0)
        gate = jnp.where(first, block[2:3], jnp.where(second, block[3:4], 0)).astype(f32)
        out_ref[k, 0:1, :] = slot
        out_ref[k, 1:2, :] = gate * gate_scale
        out_ref[k, 2:8, :] = jnp.zeros((6, width), f32)


def expert_kernel(capacity, idx_ref, slot_ref, t0, t1, t2, t3, w_in_ref, w_out_ref, keep_ref, send_ref):
    events, cols = t0.shape
    slot = slot_ref[0:1, :]
    gate = slot_ref[1:2, :]
    hit = lax.broadcasted_iota(jnp.int32, (capacity, events), 0).astype(f32) == slot
    pick = jnp.where(hit, 1.0, 0.0).astype(bf16)
    weight = jnp.where(hit, gate, 0.0).astype(bf16)
    at = [pl.ds(pl.multiple_of(idx_ref[1 + j] * cols, cols), cols) for j in range(4)]
    acc = jnp.zeros((capacity, w_in_ref.shape[1]), f32)
    for j, t in enumerate((t0, t1, t2, t3)):
        rows = jnp.dot(pick, t[...], preferred_element_type=f32).astype(bf16)
        acc = acc + jnp.dot(rows, w_in_ref[at[j], :], preferred_element_type=f32)
    hidden = jax.nn.gelu(acc).astype(bf16)
    for j, (ref, half) in enumerate(((keep_ref, 0), (send_ref, 0), (keep_ref, 1), (send_ref, 1))):
        out = jnp.dot(hidden, w_out_ref[:, at[j]], preferred_element_type=f32).astype(bf16)
        ref[:, pl.ds(half * cols, cols)] = tn(weight, out).astype(bf16)


def call(kernel, outs, *args, specs=None):
    outs = [jax.ShapeDtypeStruct(*o) for o in outs]
    single = len(outs) == 1
    return pl.pallas_call(
        kernel,
        out_shape=outs[0] if single else outs,
        in_specs=specs or [VMEM] * len(args),
        out_specs=VMEM if single else [VMEM] * len(outs),
        compiler_params=LIMIT,
    )(*args)


def swap(x, axis):
    return lax.ppermute(x, axis, [(0, 1), (1, 0)])


def turn(x, n, k):
    return lax.ppermute(x, "seq", [(i, (i + k) % n) for i in range(n)])


def later(x, n, k):
    return lax.ppermute(x, "seq", [(i, i + k) for i in range(n - k)])


def blockwise(queries, keys, values, resid, w_in, w_out, routes, gate_num):
    events, cols = queries.shape
    heads = cols // HD
    n = lax.axis_size("seq")
    capacity = 2 * TOP * events // (n * 2)
    s, m, r = lax.axis_index("seq"), lax.axis_index("mp"), lax.axis_index("rep")
    idx = jnp.stack(
        [s * 2 + r, m * 2 + r, m * 2 + 1 - r, (1 - m) * 2 + r, (1 - m) * 2 + 1 - r]
    ).astype(jnp.int32)
    first, second = w_in[0], w_out[0]

    state = call(
        functools.partial(state_kernel, heads), [((heads * HD + 16, HD), bf16)], keys, values
    )
    states = [later(state, n, k) for k in range(1, n)]

    table = jnp.concatenate(
        [routes.T, gate_num.T, jnp.zeros((8 - 2 * TOP, events), jnp.int32)], axis=0
    )
    tables = [table] + [turn(table, n, k) for k in range(1, n)]
    slots = call(
        functools.partial(route_kernel, n), [((n, 8, events), f32)], idx, *tables,
        specs=[SMEM] + [VMEM] * n,
    )
    num, den = call(
        functools.partial(local_kernel, heads),
        [((events, cols), f32), ((events, cols), f32)], queries, keys, values,
    )
    attended, squares = call(
        functools.partial(carry_kernel, heads, n - 1),
        [((events, cols), f32), ((8, events), f32)], queries, num, den, *states,
    )
    pair = squares + swap(squares, "rep")
    mixed = call(
        functools.partial(mix_kernel, 2), [((events, cols), bf16)],
        resid, attended, pair, swap(pair, "mp"),
    )
    order = [0, 2, 1, 3] if n == 4 else list(range(n))
    total = mixed.astype(f32)
    for k in order:
        mine = turn(mixed, n, k) if k else mixed
        across = swap(mine, "mp")
        keep, send = call(
            functools.partial(expert_kernel, capacity),
            [((events, 2 * cols), bf16), ((events, 2 * cols), bf16)],
            idx, slots[k], mine, swap(mine, "rep"), across, swap(across, "rep"), first, second,
            specs=[SMEM] + [VMEM] * 7,
        )
        both = keep.astype(f32) + swap(send, "rep").astype(f32)
        near, far = both[:, :cols], both[:, cols:].astype(bf16)
        part = (near + swap(far, "mp").astype(f32)).astype(bf16)
        total = total + (turn(part, n, n - k) if k else part).astype(f32)
    return total.astype(bf16)


def shards(*args):
    blocky = lax.axis_size("mp") == 2 and lax.axis_size("rep") == 2 and lax.axis_size("seq") <= 4
    return (blockwise if blocky else general)(*args)


def solution(mesh):
    in_specs = (
        P(("groups", "seq"), ("mp", "rep")),
        P(("groups", "seq"), ("mp", "rep")),
        P(("groups", "seq"), ("mp", "rep")),
        P(("groups", "seq"), ("mp", "rep")),
        P(("seq", "rep"), None, "mp"),
        P(("seq", "rep"), "mp", None),
        P(("groups", "seq"), None),
        P(("groups", "seq"), None),
    )
    out_specs = P(("groups", "seq"), ("mp", "rep"))
    return jax.shard_map(shards, mesh=mesh, in_specs=in_specs, out_specs=out_specs, check_vma=False)
```

```python
import functools

import jax
import jax.numpy as jnp
from jax import lax
from jax.experimental import pallas as pl
from jax.experimental.pallas import tpu as pltpu
from jax.sharding import PartitionSpec as P

D = 2048
HD = 128
TOP = 2

gate_scale = 1.0 / 256.0
highest = lax.Precision.HIGHEST
f32 = jnp.float32
bf16 = jnp.bfloat16
VMEM = pl.BlockSpec(memory_space=pltpu.VMEM)
SMEM = pl.BlockSpec(memory_space=pltpu.SMEM)
HBM = pl.BlockSpec(memory_space=pltpu.HBM)
LIMIT = pltpu.CompilerParams(vmem_limit_bytes=24 * 1024 * 1024)


def feature(inputs_raw):
    wide = inputs_raw.astype(f32)
    return jnp.where(wide > 0.0, wide + 1.0, jnp.exp(jnp.minimum(wide, 0.0)))


def heads_first(matrix, head_width):
    return matrix.reshape(matrix.shape[0], -1, head_width).transpose(1, 0, 2)


def general(queries, keys, values, resid, w_in, w_out, routes, gate_num):
    tok_count, col_count = queries.shape
    seq_count = lax.axis_size("seq")
    rep_count = lax.axis_size("rep")
    expert_count = seq_count * rep_count
    capacity = 2 * TOP * tok_count // expert_count
    slot_count = expert_count * capacity
    query_feat = heads_first(feature(queries), HD)
    key_feat = heads_first(feature(keys), HD)
    value_heads = heads_first(values.astype(f32), HD)
    memory = jnp.einsum("hsc,hsd->hcd", key_feat, value_heads, precision=highest)
    key_total = jnp.sum(key_feat, axis=1)
    state = jnp.concatenate([memory, key_total[:, None, :]], axis=1).astype(bf16)
    states = lax.all_gather(state, "seq").astype(f32)
    earlier = jnp.arange(seq_count) < lax.axis_index("seq")
    state = jnp.sum(jnp.where(earlier[:, None, None, None], states, 0.0), axis=0)
    before, before_total = state[:, :HD], state[:, HD]
    causal = jnp.tril(jnp.ones((tok_count, tok_count), f32))
    scores = jnp.einsum("htc,hsc->hts", query_feat, key_feat, precision=highest) * causal
    numerator = jnp.einsum("hts,hsd->htd", scores, value_heads, precision=highest)
    numerator = numerator + jnp.einsum("htc,hcd->htd", query_feat, before, precision=highest)
    denominator = jnp.sum(scores, axis=-1) + jnp.einsum(
        "htc,hc->ht", query_feat, before_total, precision=highest
    )
    attended = numerator / denominator[..., None]
    local_squares = jnp.sum(attended * attended, axis=(0, 2))
    row_squares = lax.psum(local_squares, ("mp", "rep"))
    normed = attended * lax.rsqrt(row_squares / D + 1e-06)[None, :, None]
    mixed_rows = (
        resid.astype(f32) + normed.transpose(1, 0, 2).reshape(tok_count, col_count)
    ).astype(bf16)
    routed = routes.reshape(-1)
    onehot = (routed[:, None] == jnp.arange(expert_count, dtype=jnp.int32)[None, :]).astype(f32)
    pairs = jnp.arange(tok_count * TOP)
    below = (pairs[:, None] > pairs[None, :]).astype(f32)
    counts = jnp.dot(below, onehot, precision=highest)
    slot_rank = jnp.sum(counts * onehot, axis=1).astype(jnp.int32)
    slot_index = (routed // rep_count * capacity + slot_rank) * rep_count + routed % rep_count
    matches = (slot_index[:, None] == jnp.arange(slot_count, dtype=jnp.int32)[None, :]).astype(f32)
    matches = matches.reshape(tok_count, TOP, slot_count)
    picker = jnp.sum(matches, axis=1).astype(bf16)
    weights = gate_num.astype(f32) * gate_scale
    combine = jnp.einsum("tk,tks->ts", weights, matches, precision=highest)
    outgoing = jnp.einsum("ts,tc->sc", picker, mixed_rows, preferred_element_type=f32).astype(bf16)

    def exchange(rows):
        rows = rows.reshape(seq_count, capacity, rep_count, col_count)
        rows = lax.all_to_all(rows, "seq", split_axis=0, concat_axis=0, tiled=True)
        return lax.all_to_all(rows, "rep", split_axis=2, concat_axis=2, tiled=True)

    expert_rows = exchange(outgoing).reshape(seq_count * capacity, rep_count * col_count)
    preact = jnp.dot(
        lax.all_gather(expert_rows, "mp", axis=1, tiled=True), w_in[0], preferred_element_type=f32
    )
    hidden = jax.nn.gelu(preact).astype(bf16)
    partial_value = jnp.dot(hidden, w_out[0], preferred_element_type=f32)
    summed = lax.psum_scatter(partial_value.astype(bf16), "mp", scatter_dimension=1, tiled=True)
    returned = exchange(summed).astype(f32)
    expert_mix = jnp.dot(combine, returned.reshape(slot_count, col_count), precision=highest)
    return (mixed_rows.astype(f32) + expert_mix).astype(bf16)


def nt(a, b):
    return lax.dot_general(a, b, (((1,), (1,)), ((), ())), preferred_element_type=f32)


def tn(a, b):
    return lax.dot_general(a, b, (((0,), (0,)), ((), ())), preferred_element_type=f32)


def state_kernel(heads, k_hbm, v_hbm, *refs):
    halves, (key_ref, v_ref, k_buf, sem) = refs[:2], refs[2:]
    copy_k = pltpu.make_async_copy(k_hbm, k_buf, sem.at[0])
    copy_v = pltpu.make_async_copy(v_hbm, v_ref, sem.at[1])
    copy_k.start()
    copy_v.start()
    copy_k.wait()
    copy_v.wait()
    per = heads // 2
    for half, state_ref in enumerate(halves):
        totals = []
        for i in range(per):
            cols = pl.ds((half * per + i) * HD, HD)
            key = feature(k_buf[:, cols])
            narrow = key.astype(bf16)
            key_ref[:, cols] = narrow
            state_ref[pl.ds(i * HD, HD), :] = tn(v_ref[:, cols], narrow).astype(bf16)
            totals.append(jnp.sum(key, axis=0, keepdims=True))
        totals.append(jnp.zeros((16 - per, HD), f32))
        state_ref[pl.ds(per * HD, 16), :] = jnp.concatenate(totals, axis=0).astype(bf16)


def local_kernel(heads, q_hbm, resid_hbm, key_ref, v_ref, num_ref, den_ref, query_ref, resid_ref, q_buf, sem):
    copy_q = pltpu.make_async_copy(q_hbm, q_buf, sem.at[0])
    copy_r = pltpu.make_async_copy(resid_hbm, resid_ref, sem.at[1])
    copy_q.start()
    copy_r.start()
    rows = q_buf.shape[0]
    t = lax.broadcasted_iota(jnp.int32, (rows, rows), 0)
    s = lax.broadcasted_iota(jnp.int32, (rows, rows), 1)
    copy_q.wait()
    for h in range(heads):
        cols = pl.ds(h * HD, HD)
        query = feature(q_buf[:, cols]).astype(bf16)
        query_ref[:, cols] = query
        scores = jnp.where(s <= t, nt(query, key_ref[:, cols]), 0.0).astype(bf16)
        num_ref[:, cols] = jnp.dot(scores, v_ref[:, cols], preferred_element_type=f32)
        den_ref[:, cols] = jnp.dot(scores, jnp.ones((rows, HD), bf16), preferred_element_type=f32)
    copy_r.wait()


def carry_kernel(heads, steps, query_ref, num_ref, den_ref, *refs):
    states, (att_ref, sq_ref) = refs[: 2 * steps], refs[2 * steps :]
    rows = query_ref.shape[0]
    per = heads // 2
    squares = jnp.zeros((rows, HD), f32)
    for half in range(2):
        carried = states[half][...].astype(f32)
        for step in range(1, steps):
            carried = carried + states[2 * step + half][...].astype(f32)
        carried = carried.astype(bf16)
        for i in range(per):
            cols = pl.ds((half * per + i) * HD, HD)
            query = query_ref[:, cols]
            top = num_ref[:, cols] + nt(query, carried[i * HD : (i + 1) * HD])
            total = jnp.broadcast_to(carried[per * HD + i : per * HD + i + 1], (HD, HD))
            attended = top / (den_ref[:, cols] + nt(query, total))
            att_ref[:, cols] = attended
            squares = squares + attended * attended
    sq_ref[...] = lax.dot_general(
        jnp.ones((8, HD), f32), squares, (((1,), (1,)), ((), ())),
        preferred_element_type=f32, precision=highest,
    )


def mix_kernel(resid_ref, att_ref, table_ref, *refs):
    squares, (mixed_ref, payload_ref) = refs[:-2], refs[-2:]
    rows = mixed_ref.shape[0]
    total = squares[0][...]
    for extra in squares[1:]:
        total = total + extra[...]
    column = jnp.transpose(lax.rsqrt(total * (1.0 / D) + 1e-06))[:, :1]
    mixed = (resid_ref[...].astype(f32) + att_ref[...] * column).astype(bf16)
    mixed_ref[...] = mixed
    payload_ref[pl.ds(0, rows), :] = mixed
    payload_ref[pl.ds(rows, 8), :] = table_ref[...]


def expert_kernel(capacity, idx_ref, table_ref, t0, t1, t2, t3, w_in_hbm, w_out_hbm, keep_ref, send_ref, w_in_buf, w_out_buf, sem):
    events, cols = t0.shape
    at = [pl.ds(pl.multiple_of(idx_ref[1 + j] * cols, cols), cols) for j in range(4)]
    first_in = [
        pltpu.make_async_copy(w_in_hbm.at[at[j], :], w_in_buf.at[j], sem.at[0, j]) for j in range(4)
    ]
    then_in = [
        pltpu.make_async_copy(w_out_hbm.at[:, at[j]], w_out_buf.at[j], sem.at[1, j]) for j in range(4)
    ]
    for copy in first_in + then_in:
        copy.start()
    table = table_ref[...].astype(f32)[:, :events]
    expert = idx_ref[0].astype(f32)
    first, second = table[0:1] == expert, table[1:2] == expert
    named = first | second
    gate = jnp.where(first, table[2:3], table[3:4]) * gate_scale
    a = lax.broadcasted_iota(jnp.int32, (events, events), 0)
    b = lax.broadcasted_iota(jnp.int32, (events, events), 1)
    flag = jnp.broadcast_to(jnp.where(named, 1.0, 0.0), (8, events)).astype(bf16)
    rank = jnp.dot(flag, jnp.where(a < b, 1.0, 0.0).astype(bf16), preferred_element_type=f32)
    slot = jnp.where(named, rank[0:1], -1.0)
    hit = lax.broadcasted_iota(jnp.int32, (capacity, events), 0).astype(f32) == slot
    pick = jnp.where(hit, 1.0, 0.0).astype(bf16)
    weight = jnp.where(hit, gate, 0.0).astype(bf16)
    acc = jnp.zeros((capacity, w_in_hbm.shape[1]), f32)
    for j, t in enumerate((t0, t1, t2, t3)):
        rows = jnp.dot(pick, t[...], preferred_element_type=f32).astype(bf16)
        first_in[j].wait()
        acc = acc + jnp.dot(rows, w_in_buf[j], preferred_element_type=f32)
    hidden = jax.nn.gelu(acc).astype(bf16)
    for j, (ref, half) in enumerate(((keep_ref, 0), (send_ref, 0), (keep_ref, 1), (send_ref, 1))):
        then_in[j].wait()
        out = jnp.dot(hidden, w_out_buf[j], preferred_element_type=f32).astype(bf16)
        ref[:, pl.ds(half * cols, cols)] = tn(weight, out).astype(bf16)


def call(kernel, outs, *args, specs=None, scratch=()):
    outs = [jax.ShapeDtypeStruct(*o) for o in outs]
    single = len(outs) == 1
    return pl.pallas_call(
        kernel,
        out_shape=outs[0] if single else outs,
        in_specs=specs or [VMEM] * len(args),
        out_specs=VMEM if single else [VMEM] * len(outs),
        scratch_shapes=scratch,
        compiler_params=LIMIT,
    )(*args)


def far_off(*arrays):
    return [pltpu.with_memory_space_constraint(x, pltpu.HBM) for x in arrays]


def swap(x, *axes):
    if len(axes) == 1:
        return lax.ppermute(x, axes[0], [(0, 1), (1, 0)])
    return lax.ppermute(x, axes, [(i, 3 - i) for i in range(4)])


def turn(x, n, k):
    return lax.ppermute(x, "seq", [(i, (i + k) % n) for i in range(n)])


def later(x, n, k):
    return lax.ppermute(x, "seq", [(i, i + k) for i in range(n - k)])


def added(a, b):
    return (a.astype(f32) + b.astype(f32)).astype(bf16)


def after(x, *others):
    return lax.optimization_barrier((x, *others))[0]


def blockwise(queries, keys, values, resid, w_in, w_out, routes, gate_num):
    events, cols = queries.shape
    heads = cols // HD
    n = lax.axis_size("seq")
    capacity = 2 * TOP * events // (n * 2)
    s, m, r = lax.axis_index("seq"), lax.axis_index("mp"), lax.axis_index("rep")
    idx = jnp.stack(
        [s * 2 + r, m * 2 + r, m * 2 + 1 - r, (1 - m) * 2 + r, (1 - m) * 2 + 1 - r]
    ).astype(jnp.int32)
    wide, narrow = ((events, cols), f32), ((events, cols), bf16)
    state_shape = ((heads // 2 * HD + 16, HD), bf16)
    buffer = [pltpu.VMEM((events, cols), bf16), pltpu.SemaphoreType.DMA((2,))]

    *state, key, value = call(
        functools.partial(state_kernel, heads), [state_shape, state_shape, narrow, narrow],
        *far_off(keys, values), specs=[HBM] * 2, scratch=buffer,
    )
    states = [later(x, n, 1) for x in state]
    num, den, query, resid_near = call(
        functools.partial(local_kernel, heads), [wide, wide, narrow, narrow],
        *far_off(queries, resid), key, value, specs=[HBM] * 2 + [VMEM] * 2, scratch=buffer,
    )
    if n > 2:
        second = [
            later((own.astype(f32) + one.astype(f32)).astype(bf16), n, 2)
            for own, one in zip(state, states)
        ]
        states = [*states, *second]
    table = jnp.concatenate([routes.T, gate_num.T], axis=0).astype(bf16)
    table = jnp.pad(table, ((0, 8 - 2 * TOP), (0, cols - events)))
    attended, squares = call(
        functools.partial(carry_kernel, heads, len(states) // 2), [wide, ((8, events), f32)],
        query, num, den, *states,
    )
    mixed, payload = call(
        mix_kernel, [narrow, ((events + 8, cols), bf16)], resid_near, attended, table,
        squares, swap(squares, "rep"), swap(squares, "mp"), swap(squares, "mp", "rep"),
    )

    weights = far_off(w_in[0], w_out[0])
    hidden = w_in.shape[2]

    def expert(block, mine, across, behind):
        beside, corner = swap(mine, "rep"), swap(across, "rep")
        keep, send = call(
            functools.partial(expert_kernel, capacity), [((events, 2 * cols), bf16)] * 2,
            idx, lax.slice_in_dim(block, events, events + 8), mine, beside, across,
            after(corner, *behind), *weights,
            specs=[SMEM] + [VMEM] * 5 + [HBM] * 2,
            scratch=[
                pltpu.VMEM((4, cols, hidden), bf16), pltpu.VMEM((4, hidden, cols), bf16),
                pltpu.SemaphoreType.DMA((2, 4)),
            ],
        )
        both = keep.astype(f32) + swap(send, "rep").astype(f32)
        return send, both[:, :cols].astype(bf16), both[:, cols:].astype(bf16)

    def joined(near, far):
        return (near.astype(f32) + swap(far, "mp").astype(f32)).astype(bf16)

    across = swap(mixed, "mp")
    send, near, far = expert(payload, mixed, across, ())
    parts, block, sums = [joined(near, far)], payload, None
    for k in range(1, n):
        block = turn(block, n, 1)
        mine = lax.slice_in_dim(block, 0, events)
        across = swap(after(mine, across), "mp")
        behind = (send, far) if k > 1 else (send,)
        send, near, far = expert(block, mine, across, (*behind, *parts[:-1]))
        parts.append(joined(near, far))
        sums = turn(parts[k] if sums is None else added(parts[k], sums), n, 1)
    total = mixed.astype(f32) + parts[0].astype(f32)
    if sums is not None:
        total = total + sums.astype(f32)
    return total.astype(bf16)


def shards(*args):
    blocky = lax.axis_size("mp") == 2 and lax.axis_size("rep") == 2 and lax.axis_size("seq") <= 4
    return (blockwise if blocky else general)(*args)


def solution(mesh):
    in_specs = (
        P(("groups", "seq"), ("mp", "rep")),
        P(("groups", "seq"), ("mp", "rep")),
        P(("groups", "seq"), ("mp", "rep")),
        P(("groups", "seq"), ("mp", "rep")),
        P(("seq", "rep"), None, "mp"),
        P(("seq", "rep"), "mp", None),
        P(("groups", "seq"), None),
        P(("groups", "seq"), None),
    )
    out_specs = P(("groups", "seq"), ("mp", "rep"))
    return jax.shard_map(shards, mesh=mesh, in_specs=in_specs, out_specs=out_specs, check_vma=False)
```

```python
import functools

import jax
import jax.numpy as jnp
from jax import lax
from jax.experimental import pallas as pl
from jax.experimental.pallas import tpu as pltpu
from jax.sharding import PartitionSpec as P

D = 2048
HD = 128
TOP = 2

STEPS = (
    ("z", 1),
    ("z", 2),
    ("z", 3),
    ("x", 0),
    ("x", 1),
    ("x", 2),
    ("x", 3),
    ("k", 0),
    ("k", 1),
    ("f", 0),
    ("k", 3),
    ("k", 2),
    ("f", 1),
    ("f", 2),
    ("f", 3),
    ("p", 0),
    ("p", 2),
    ("p", 1),
    ("p", 3),
)
WAITS = {
    ("k", 1): (("k", 0),),
    ("k", 3): (("k", 1), ("f", 0)),
    ("k", 2): (("k", 3),),
}


gate_scale = 1.0 / 256.0
highest = lax.Precision.HIGHEST
f32 = jnp.float32
bf16 = jnp.bfloat16
VMEM = pl.BlockSpec(memory_space=pltpu.VMEM)
SMEM = pl.BlockSpec(memory_space=pltpu.SMEM)
HBM = pl.BlockSpec(memory_space=pltpu.HBM)
LIMIT = pltpu.CompilerParams(vmem_limit_bytes=24 * 1024 * 1024)


def feature(inputs_raw):
    wide = inputs_raw.astype(f32)
    return jnp.where(wide > 0.0, wide + 1.0, jnp.exp(jnp.minimum(wide, 0.0)))


def heads_first(matrix, head_width):
    return matrix.reshape(matrix.shape[0], -1, head_width).transpose(1, 0, 2)


def general(queries, keys, values, resid, w_in, w_out, routes, gate_num):
    tok_count, col_count = queries.shape
    seq_count = lax.axis_size("seq")
    rep_count = lax.axis_size("rep")
    expert_count = seq_count * rep_count
    capacity = 2 * TOP * tok_count // expert_count
    slot_count = expert_count * capacity
    query_feat = heads_first(feature(queries), HD)
    key_feat = heads_first(feature(keys), HD)
    value_heads = heads_first(values.astype(f32), HD)
    memory = jnp.einsum("hsc,hsd->hcd", key_feat, value_heads, precision=highest)
    key_total = jnp.sum(key_feat, axis=1)
    state = jnp.concatenate([memory, key_total[:, None, :]], axis=1).astype(bf16)
    states = lax.all_gather(state, "seq").astype(f32)
    earlier = jnp.arange(seq_count) < lax.axis_index("seq")
    state = jnp.sum(jnp.where(earlier[:, None, None, None], states, 0.0), axis=0)
    before, before_total = state[:, :HD], state[:, HD]
    causal = jnp.tril(jnp.ones((tok_count, tok_count), f32))
    scores = jnp.einsum("htc,hsc->hts", query_feat, key_feat, precision=highest) * causal
    numerator = jnp.einsum("hts,hsd->htd", scores, value_heads, precision=highest)
    numerator = numerator + jnp.einsum("htc,hcd->htd", query_feat, before, precision=highest)
    denominator = jnp.sum(scores, axis=-1) + jnp.einsum(
        "htc,hc->ht", query_feat, before_total, precision=highest
    )
    attended = numerator / denominator[..., None]
    local_squares = jnp.sum(attended * attended, axis=(0, 2))
    row_squares = lax.psum(local_squares, ("mp", "rep"))
    normed = attended * lax.rsqrt(row_squares / D + 1e-06)[None, :, None]
    mixed_rows = (
        resid.astype(f32) + normed.transpose(1, 0, 2).reshape(tok_count, col_count)
    ).astype(bf16)
    routed = routes.reshape(-1)
    onehot = (routed[:, None] == jnp.arange(expert_count, dtype=jnp.int32)[None, :]).astype(f32)
    pairs = jnp.arange(tok_count * TOP)
    below = (pairs[:, None] > pairs[None, :]).astype(f32)
    counts = jnp.dot(below, onehot, precision=highest)
    slot_rank = jnp.sum(counts * onehot, axis=1).astype(jnp.int32)
    slot_index = (routed // rep_count * capacity + slot_rank) * rep_count + routed % rep_count
    matches = (slot_index[:, None] == jnp.arange(slot_count, dtype=jnp.int32)[None, :]).astype(f32)
    matches = matches.reshape(tok_count, TOP, slot_count)
    picker = jnp.sum(matches, axis=1).astype(bf16)
    weights = gate_num.astype(f32) * gate_scale
    combine = jnp.einsum("tk,tks->ts", weights, matches, precision=highest)
    outgoing = jnp.einsum("ts,tc->sc", picker, mixed_rows, preferred_element_type=f32).astype(bf16)

    def exchange(rows):
        rows = rows.reshape(seq_count, capacity, rep_count, col_count)
        rows = lax.all_to_all(rows, "seq", split_axis=0, concat_axis=0, tiled=True)
        return lax.all_to_all(rows, "rep", split_axis=2, concat_axis=2, tiled=True)

    expert_rows = exchange(outgoing).reshape(seq_count * capacity, rep_count * col_count)
    preact = jnp.dot(
        lax.all_gather(expert_rows, "mp", axis=1, tiled=True), w_in[0], preferred_element_type=f32
    )
    hidden = jax.nn.gelu(preact).astype(bf16)
    partial_value = jnp.dot(hidden, w_out[0], preferred_element_type=f32)
    summed = lax.psum_scatter(partial_value.astype(bf16), "mp", scatter_dimension=1, tiled=True)
    returned = exchange(summed).astype(f32)
    expert_mix = jnp.dot(combine, returned.reshape(slot_count, col_count), precision=highest)
    return (mixed_rows.astype(f32) + expert_mix).astype(bf16)


def nt(a, b):
    return lax.dot_general(a, b, (((1,), (1,)), ((), ())), preferred_element_type=f32)


def tn(a, b):
    return lax.dot_general(a, b, (((0,), (0,)), ((), ())), preferred_element_type=f32)


def state_kernel(heads, k_hbm, v_hbm, state_ref, key_ref, v_ref, k_buf, sem):
    copy_k = pltpu.make_async_copy(k_hbm, k_buf, sem.at[0])
    copy_v = pltpu.make_async_copy(v_hbm, v_ref, sem.at[1])
    copy_k.start()
    copy_v.start()
    copy_k.wait()
    copy_v.wait()
    totals = []
    for h in range(heads):
        cols = pl.ds(h * HD, HD)
        key = feature(k_buf[:, cols])
        narrow = key.astype(bf16)
        key_ref[:, cols] = narrow
        state_ref[pl.ds(h * HD, HD), :] = tn(v_ref[:, cols], narrow).astype(bf16)
        totals.append(jnp.sum(key, axis=0, keepdims=True))
    totals.append(jnp.zeros((16 - heads, HD), f32))
    state_ref[pl.ds(heads * HD, 16), :] = jnp.concatenate(totals, axis=0).astype(bf16)


def local_kernel(heads, q_hbm, resid_hbm, key_ref, v_ref, num_ref, den_ref, query_ref, resid_ref, q_buf, sem):
    copy_q = pltpu.make_async_copy(q_hbm, q_buf, sem.at[0])
    copy_r = pltpu.make_async_copy(resid_hbm, resid_ref, sem.at[1])
    copy_q.start()
    copy_r.start()
    rows = q_buf.shape[0]
    t = lax.broadcasted_iota(jnp.int32, (rows, rows), 0)
    s = lax.broadcasted_iota(jnp.int32, (rows, rows), 1)
    copy_q.wait()
    for h in range(heads):
        cols = pl.ds(h * HD, HD)
        query = feature(q_buf[:, cols]).astype(bf16)
        query_ref[:, cols] = query
        scores = jnp.where(s <= t, nt(query, key_ref[:, cols]), 0.0).astype(bf16)
        num_ref[:, cols] = jnp.dot(scores, v_ref[:, cols], preferred_element_type=f32)
        den_ref[:, cols] = jnp.dot(scores, jnp.ones((rows, HD), bf16), preferred_element_type=f32)
    copy_r.wait()


def carry_kernel(heads, query_ref, num_ref, den_ref, *refs):
    states, (att_ref, sq_ref) = refs[:-2], refs[-2:]
    squares = jnp.zeros((query_ref.shape[0], HD), f32)
    carried = states[0][...].astype(f32)
    for extra in states[1:]:
        carried = carried + extra[...].astype(f32)
    carried = carried.astype(bf16)
    for h in range(heads):
        cols = pl.ds(h * HD, HD)
        query = query_ref[:, cols]
        top = num_ref[:, cols] + nt(query, carried[h * HD : (h + 1) * HD])
        total = jnp.broadcast_to(carried[heads * HD + h : heads * HD + h + 1], (HD, HD))
        attended = top / (den_ref[:, cols] + nt(query, total))
        att_ref[:, cols] = attended
        squares = squares + attended * attended
    sq_ref[...] = lax.dot_general(
        jnp.ones((8, HD), f32), squares, (((1,), (1,)), ((), ())),
        preferred_element_type=f32, precision=highest,
    )


def mix_kernel(resid_ref, att_ref, table_ref, *refs):
    squares, (mixed_ref, payload_ref) = refs[:-2], refs[-2:]
    rows = mixed_ref.shape[0]
    total = squares[0][...]
    for extra in squares[1:]:
        total = total + extra[...]
    column = jnp.transpose(lax.rsqrt(total * (1.0 / D) + 1e-06))[:, :1]
    mixed = (resid_ref[...].astype(f32) + att_ref[...] * column).astype(bf16)
    mixed_ref[...] = mixed
    payload_ref[pl.ds(0, rows), :] = mixed
    payload_ref[pl.ds(rows, 8), :] = table_ref[...]


def expert_kernel(capacity, idx_ref, table_ref, t0, t1, t2, t3, w_in_hbm, w_out_hbm, keep_ref, send_ref, w_in_buf, w_out_buf, sem):
    events, cols = t0.shape
    at = [pl.ds(pl.multiple_of(idx_ref[1 + j] * cols, cols), cols) for j in range(4)]
    first_in = [
        pltpu.make_async_copy(w_in_hbm.at[at[j], :], w_in_buf.at[j], sem.at[0, j]) for j in range(4)
    ]
    then_in = [
        pltpu.make_async_copy(w_out_hbm.at[:, at[j]], w_out_buf.at[j], sem.at[1, j]) for j in range(4)
    ]
    for copy in first_in + then_in:
        copy.start()
    table = table_ref[...].astype(f32)[:, :events]
    expert = idx_ref[0].astype(f32)
    first, second = table[0:1] == expert, table[1:2] == expert
    named = first | second
    gate = jnp.where(first, table[2:3], table[3:4]) * gate_scale
    a = lax.broadcasted_iota(jnp.int32, (events, events), 0)
    b = lax.broadcasted_iota(jnp.int32, (events, events), 1)
    flag = jnp.broadcast_to(jnp.where(named, 1.0, 0.0), (8, events)).astype(bf16)
    rank = jnp.dot(flag, jnp.where(a < b, 1.0, 0.0).astype(bf16), preferred_element_type=f32)
    slot = jnp.where(named, rank[0:1], -1.0)
    hit = lax.broadcasted_iota(jnp.int32, (capacity, events), 0).astype(f32) == slot
    pick = jnp.where(hit, 1.0, 0.0).astype(bf16)
    weight = jnp.where(hit, gate, 0.0).astype(bf16)
    acc = jnp.zeros((capacity, w_in_hbm.shape[1]), f32)
    for j, t in enumerate((t0, t1, t2, t3)):
        rows = jnp.dot(pick, t[...], preferred_element_type=f32).astype(bf16)
        first_in[j].wait()
        acc = acc + jnp.dot(rows, w_in_buf[j], preferred_element_type=f32)
    hidden = jax.nn.gelu(acc).astype(bf16)
    for j, (ref, half) in enumerate(((keep_ref, 0), (send_ref, 0), (keep_ref, 1), (send_ref, 1))):
        then_in[j].wait()
        out = jnp.dot(hidden, w_out_buf[j], preferred_element_type=f32).astype(bf16)
        ref[:, pl.ds(half * cols, cols)] = tn(weight, out).astype(bf16)


def call(kernel, outs, *args, specs=None, scratch=(), flops=0, moved=0):
    outs = [jax.ShapeDtypeStruct(*o) for o in outs]
    single = len(outs) == 1
    return pl.pallas_call(
        kernel,
        out_shape=outs[0] if single else outs,
        in_specs=specs or [VMEM] * len(args),
        out_specs=VMEM if single else [VMEM] * len(outs),
        scratch_shapes=scratch,
        cost_estimate=pl.CostEstimate(flops=flops, bytes_accessed=moved, transcendentals=0) if flops else None,
        compiler_params=LIMIT,
    )(*args)


def far_off(*arrays):
    return [pltpu.with_memory_space_constraint(x, pltpu.HBM) for x in arrays]


def swap(x, *axes):
    if len(axes) == 1:
        return lax.ppermute(x, axes[0], [(0, 1), (1, 0)])
    return lax.ppermute(x, axes, [(i, 3 - i) for i in range(4)])


def turn(x, n, k):
    return lax.ppermute(x, "seq", [(i, (i + k) % n) for i in range(n)])


def later(x, n, k):
    return lax.ppermute(x, "seq", [(i, i + k) for i in range(n - k)])


def added(a, b):
    return (a.astype(f32) + b.astype(f32)).astype(bf16)


def after(x, *others):
    return lax.optimization_barrier((x, *others))[0]


def blockwise(queries, keys, values, resid, w_in, w_out, routes, gate_num):
    events, cols = queries.shape
    heads = cols // HD
    n = lax.axis_size("seq")
    capacity = 2 * TOP * events // (n * 2)
    s, m, r = lax.axis_index("seq"), lax.axis_index("mp"), lax.axis_index("rep")
    idx = jnp.stack(
        [s * 2 + r, m * 2 + r, m * 2 + 1 - r, (1 - m) * 2 + r, (1 - m) * 2 + 1 - r]
    ).astype(jnp.int32)
    wide, narrow = ((events, cols), f32), ((events, cols), bf16)
    buffer = [pltpu.VMEM((events, cols), bf16), pltpu.SemaphoreType.DMA((2,))]

    state, key, value = call(
        functools.partial(state_kernel, heads), [((heads * HD + 16, HD), bf16), narrow, narrow],
        *far_off(keys, values), specs=[HBM] * 2, scratch=buffer,
    )
    states = [later(state, n, k) for k in range(1, n)]
    num, den, query, resid_near = call(
        functools.partial(local_kernel, heads), [wide, wide, narrow, narrow],
        *far_off(queries, resid), key, value, specs=[HBM] * 2 + [VMEM] * 2, scratch=buffer,
    )
    table = jnp.concatenate([routes.T, gate_num.T], axis=0).astype(bf16)
    table = jnp.pad(table, ((0, 8 - 2 * TOP), (0, cols - events)))
    attended, squares = call(
        functools.partial(carry_kernel, heads), [wide, ((8, events), f32)],
        query, num, den, *states,
    )
    mixed, payload = call(
        mix_kernel, [narrow, ((events + 8, cols), bf16)], resid_near, attended, table,
        squares, swap(squares, "rep"), swap(squares, "mp"), swap(squares, "mp", "rep"),
    )

    weights = far_off(w_in[0], w_out[0])
    hidden = w_in.shape[2]

    mine, table, across, beside, corner = {}, {}, {}, {}, {}
    arrived, send, keep, back, near, far, cross, part, home = {}, {}, {}, {}, {}, {}, {}, {}, {}

    def received(k, block):
        mine[k] = mixed if k == 0 else lax.slice_in_dim(block, 0, events)
        table[k] = lax.slice_in_dim(block, events, events + 8)
        across[k], beside[k] = swap(mine[k], "mp"), swap(mine[k], "rep")

    for k in (1, 3):
        arrived[k] = turn(payload, n, k)
    received(0, payload)
    vals = {}
    def gate(x, step, k):
        deps = [vals[d] for d in WAITS.get((step, k), ())]
        return after(x, *deps) if deps else x
    for step, k in STEPS:
        if step == "z":
            last = gate(arrived[k], step, k)
            received(k, last)
            if k == 1:
                arrived[2] = turn(last, n, (2 - k) % n)
        elif step == "x":
            across[k] = last = gate(across[k], step, k)
            corner[k] = swap(last, "rep")
        elif step == "k":
            keep[k], send[k] = call(
                functools.partial(expert_kernel, capacity), [((events, 2 * cols), bf16)] * 2,
                idx, table[k], mine[k], beside[k], across[k], gate(corner[k], step, k), *weights,
                specs=[SMEM] + [VMEM] * 5 + [HBM] * 2,
                scratch=[
                    pltpu.VMEM((4, cols, hidden), bf16), pltpu.VMEM((4, hidden, cols), bf16),
                    pltpu.SemaphoreType.DMA((2, 4)),
                ],
                flops=8 * capacity * cols * (2 * events + 2 * hidden), moved=4 * w_in.size,
            )
            last = send[k]
            back[k] = swap(last, "rep")
        elif step == "f":
            both = keep[k].astype(f32) + gate(back[k], step, k).astype(f32)
            near[k], far[k] = both[:, :cols].astype(bf16), both[:, cols:].astype(bf16)
            last = far[k]
            cross[k] = swap(last, "mp")
        else:
            whole = near[k].astype(f32) + gate(cross[k], step, k).astype(f32)
            if k == 1:
                whole = whole + home.pop(2).astype(f32)
            part[k] = last = whole.astype(bf16)
            if k:
                home[k] = turn(last, n, (1 - k) % n if k == 2 else n - k)
        vals[(step, k)] = last
    total = mixed.astype(f32) + part[0].astype(f32)
    for x in home.values():
        total = total + x.astype(f32)
    return total.astype(bf16)


def shards(*args):
    blocky = lax.axis_size("mp") == 2 and lax.axis_size("rep") == 2 and lax.axis_size("seq") == 4
    return (blockwise if blocky else general)(*args)


def solution(mesh):
    in_specs = (
        P(("groups", "seq"), ("mp", "rep")),
        P(("groups", "seq"), ("mp", "rep")),
        P(("groups", "seq"), ("mp", "rep")),
        P(("groups", "seq"), ("mp", "rep")),
        P(("seq", "rep"), None, "mp"),
        P(("seq", "rep"), "mp", None),
        P(("groups", "seq"), None),
        P(("groups", "seq"), None),
    )
    out_specs = P(("groups", "seq"), ("mp", "rep"))
    return jax.shard_map(shards, mesh=mesh, in_specs=in_specs, out_specs=out_specs, check_vma=False)
```

```python
import functools

import jax
import jax.numpy as jnp
from jax import lax
from jax.experimental import pallas as pl
from jax.experimental.pallas import tpu as pltpu
from jax.sharding import PartitionSpec as P

D = 2048
HD = 128
TOP = 2

STEPS = (
    ("z", 1),
    ("z", 3),
    ("x", 0),
    ("x", 3),
    ("x", 1),
    ("k", 0),
    ("z", 2),
    ("x", 2),
    ("k", 3),
    ("f", 0),
    ("k", 1),
    ("f", 1),
    ("f", 3),
    ("k", 2),
    ("f", 2),
    ("p", 0),
    ("p", 2),
    ("p", 3),
    ("p", 1),
)
WAITS = {
    ("k", 1): (("f", 0), ("x", 2)),
    ("z", 2): (("k", 0),),
    ("k", 2): (("x", 2), ("x", 0)),
    ("f", 2): (("z", 3), ("k", 1)),
    ("x", 3): (("z", 1),),
    ("x", 1): (("x", 3),),
}


gate_scale = 1.0 / 256.0
highest = lax.Precision.HIGHEST
f32 = jnp.float32
bf16 = jnp.bfloat16
VMEM = pl.BlockSpec(memory_space=pltpu.VMEM)
SMEM = pl.BlockSpec(memory_space=pltpu.SMEM)
HBM = pl.BlockSpec(memory_space=pltpu.HBM)
LIMIT = pltpu.CompilerParams(vmem_limit_bytes=24 * 1024 * 1024)


def feature(inputs_raw):
    wide = inputs_raw.astype(f32)
    return jnp.where(wide > 0.0, wide + 1.0, jnp.exp(jnp.minimum(wide, 0.0)))


def heads_first(matrix, head_width):
    return matrix.reshape(matrix.shape[0], -1, head_width).transpose(1, 0, 2)


def general(queries, keys, values, resid, w_in, w_out, routes, gate_num):
    tok_count, col_count = queries.shape
    seq_count = lax.axis_size("seq")
    rep_count = lax.axis_size("rep")
    expert_count = seq_count * rep_count
    capacity = 2 * TOP * tok_count // expert_count
    slot_count = expert_count * capacity
    query_feat = heads_first(feature(queries), HD)
    key_feat = heads_first(feature(keys), HD)
    value_heads = heads_first(values.astype(f32), HD)
    memory = jnp.einsum("hsc,hsd->hcd", key_feat, value_heads, precision=highest)
    key_total = jnp.sum(key_feat, axis=1)
    state = jnp.concatenate([memory, key_total[:, None, :]], axis=1).astype(bf16)
    states = lax.all_gather(state, "seq").astype(f32)
    earlier = jnp.arange(seq_count) < lax.axis_index("seq")
    state = jnp.sum(jnp.where(earlier[:, None, None, None], states, 0.0), axis=0)
    before, before_total = state[:, :HD], state[:, HD]
    causal = jnp.tril(jnp.ones((tok_count, tok_count), f32))
    scores = jnp.einsum("htc,hsc->hts", query_feat, key_feat, precision=highest) * causal
    numerator = jnp.einsum("hts,hsd->htd", scores, value_heads, precision=highest)
    numerator = numerator + jnp.einsum("htc,hcd->htd", query_feat, before, precision=highest)
    denominator = jnp.sum(scores, axis=-1) + jnp.einsum(
        "htc,hc->ht", query_feat, before_total, precision=highest
    )
    attended = numerator / denominator[..., None]
    local_squares = jnp.sum(attended * attended, axis=(0, 2))
    row_squares = lax.psum(local_squares, ("mp", "rep"))
    normed = attended * lax.rsqrt(row_squares / D + 1e-06)[None, :, None]
    mixed_rows = (
        resid.astype(f32) + normed.transpose(1, 0, 2).reshape(tok_count, col_count)
    ).astype(bf16)
    routed = routes.reshape(-1)
    onehot = (routed[:, None] == jnp.arange(expert_count, dtype=jnp.int32)[None, :]).astype(f32)
    pairs = jnp.arange(tok_count * TOP)
    below = (pairs[:, None] > pairs[None, :]).astype(f32)
    counts = jnp.dot(below, onehot, precision=highest)
    slot_rank = jnp.sum(counts * onehot, axis=1).astype(jnp.int32)
    slot_index = (routed // rep_count * capacity + slot_rank) * rep_count + routed % rep_count
    matches = (slot_index[:, None] == jnp.arange(slot_count, dtype=jnp.int32)[None, :]).astype(f32)
    matches = matches.reshape(tok_count, TOP, slot_count)
    picker = jnp.sum(matches, axis=1).astype(bf16)
    weights = gate_num.astype(f32) * gate_scale
    combine = jnp.einsum("tk,tks->ts", weights, matches, precision=highest)
    outgoing = jnp.einsum("ts,tc->sc", picker, mixed_rows, preferred_element_type=f32).astype(bf16)

    def exchange(rows):
        rows = rows.reshape(seq_count, capacity, rep_count, col_count)
        rows = lax.all_to_all(rows, "seq", split_axis=0, concat_axis=0, tiled=True)
        return lax.all_to_all(rows, "rep", split_axis=2, concat_axis=2, tiled=True)

    expert_rows = exchange(outgoing).reshape(seq_count * capacity, rep_count * col_count)
    preact = jnp.dot(
        lax.all_gather(expert_rows, "mp", axis=1, tiled=True), w_in[0], preferred_element_type=f32
    )
    hidden = jax.nn.gelu(preact).astype(bf16)
    partial_value = jnp.dot(hidden, w_out[0], preferred_element_type=f32)
    summed = lax.psum_scatter(partial_value.astype(bf16), "mp", scatter_dimension=1, tiled=True)
    returned = exchange(summed).astype(f32)
    expert_mix = jnp.dot(combine, returned.reshape(slot_count, col_count), precision=highest)
    return (mixed_rows.astype(f32) + expert_mix).astype(bf16)


def nt(a, b):
    return lax.dot_general(a, b, (((1,), (1,)), ((), ())), preferred_element_type=f32)


def tn(a, b):
    return lax.dot_general(a, b, (((0,), (0,)), ((), ())), preferred_element_type=f32)


def state_kernel(heads, k_hbm, v_hbm, state_ref, key_ref, v_ref, k_buf, sem):
    copy_k = pltpu.make_async_copy(k_hbm, k_buf, sem.at[0])
    copy_v = pltpu.make_async_copy(v_hbm, v_ref, sem.at[1])
    copy_k.start()
    copy_v.start()
    copy_k.wait()
    copy_v.wait()
    totals = []
    for h in range(heads):
        cols = pl.ds(h * HD, HD)
        key = feature(k_buf[:, cols])
        narrow = key.astype(bf16)
        key_ref[:, cols] = narrow
        state_ref[pl.ds(h * HD, HD), :] = tn(v_ref[:, cols], narrow).astype(bf16)
        totals.append(jnp.sum(key, axis=0, keepdims=True))
    totals.append(jnp.zeros((16 - heads, HD), f32))
    state_ref[pl.ds(heads * HD, 16), :] = jnp.concatenate(totals, axis=0).astype(bf16)


def local_kernel(heads, q_hbm, resid_hbm, key_ref, v_ref, num_ref, den_ref, query_ref, resid_ref, q_buf, sem):
    copy_q = pltpu.make_async_copy(q_hbm, q_buf, sem.at[0])
    copy_r = pltpu.make_async_copy(resid_hbm, resid_ref, sem.at[1])
    copy_q.start()
    copy_r.start()
    rows = q_buf.shape[0]
    t = lax.broadcasted_iota(jnp.int32, (rows, rows), 0)
    s = lax.broadcasted_iota(jnp.int32, (rows, rows), 1)
    copy_q.wait()
    for h in range(heads):
        cols = pl.ds(h * HD, HD)
        query = feature(q_buf[:, cols]).astype(bf16)
        query_ref[:, cols] = query
        scores = jnp.where(s <= t, nt(query, key_ref[:, cols]), 0.0).astype(bf16)
        num_ref[:, cols] = jnp.dot(scores, v_ref[:, cols], preferred_element_type=f32)
        den_ref[:, cols] = jnp.dot(scores, jnp.ones((rows, HD), bf16), preferred_element_type=f32)
    copy_r.wait()


def carry_kernel(heads, query_ref, num_ref, den_ref, *refs):
    states, (att_ref, sq_ref) = refs[:-2], refs[-2:]
    squares = jnp.zeros((query_ref.shape[0], HD), f32)
    carried = states[0][...].astype(f32)
    for extra in states[1:]:
        carried = carried + extra[...].astype(f32)
    carried = carried.astype(bf16)
    for h in range(heads):
        cols = pl.ds(h * HD, HD)
        query = query_ref[:, cols]
        top = num_ref[:, cols] + nt(query, carried[h * HD : (h + 1) * HD])
        total = jnp.broadcast_to(carried[heads * HD + h : heads * HD + h + 1], (HD, HD))
        attended = top / (den_ref[:, cols] + nt(query, total))
        att_ref[:, cols] = attended
        squares = squares + attended * attended
    sq_ref[...] = lax.dot_general(
        jnp.ones((8, HD), f32), squares, (((1,), (1,)), ((), ())),
        preferred_element_type=f32, precision=highest,
    )


def mix_kernel(resid_ref, att_ref, table_ref, *refs):
    squares, (mixed_ref, payload_ref) = refs[:-2], refs[-2:]
    rows = mixed_ref.shape[0]
    total = squares[0][...]
    for extra in squares[1:]:
        total = total + extra[...]
    column = jnp.transpose(lax.rsqrt(total * (1.0 / D) + 1e-06))[:, :1]
    mixed = (resid_ref[...].astype(f32) + att_ref[...] * column).astype(bf16)
    mixed_ref[...] = mixed
    payload_ref[pl.ds(0, rows), :] = mixed
    payload_ref[pl.ds(rows, 8), :] = table_ref[...]


def expert_kernel(capacity, idx_ref, table_ref, t0, t1, t2, t3, w_in_ref, w_out_ref, keep_ref, send_ref):
    events, cols = t0.shape
    at = [pl.ds(pl.multiple_of(idx_ref[1 + j] * cols, cols), cols) for j in range(4)]
    table = table_ref[...].astype(f32)[:, :events]
    expert = idx_ref[0].astype(f32)
    first, second = table[0:1] == expert, table[1:2] == expert
    named = first | second
    gate = jnp.where(first, table[2:3], table[3:4]) * gate_scale
    a = lax.broadcasted_iota(jnp.int32, (events, events), 0)
    b = lax.broadcasted_iota(jnp.int32, (events, events), 1)
    flag = jnp.broadcast_to(jnp.where(named, 1.0, 0.0), (8, events)).astype(bf16)
    rank = jnp.dot(flag, jnp.where(a < b, 1.0, 0.0).astype(bf16), preferred_element_type=f32)
    slot = jnp.where(named, rank[0:1], -1.0)
    hit = lax.broadcasted_iota(jnp.int32, (capacity, events), 0).astype(f32) == slot
    pick = jnp.where(hit, 1.0, 0.0).astype(bf16)
    weight = jnp.where(hit, gate, 0.0).astype(bf16)
    acc = jnp.zeros((capacity, w_in_ref.shape[1]), f32)
    for j, t in enumerate((t0, t1, t2, t3)):
        rows = jnp.dot(pick, t[...], preferred_element_type=f32).astype(bf16)
        acc = acc + jnp.dot(rows, w_in_ref[at[j], :], preferred_element_type=f32)
    hidden = jax.nn.gelu(acc).astype(bf16)
    for j, (ref, half) in enumerate(((keep_ref, 0), (send_ref, 0), (keep_ref, 1), (send_ref, 1))):
        out = jnp.dot(hidden, w_out_ref[:, at[j]], preferred_element_type=f32).astype(bf16)
        ref[:, pl.ds(half * cols, cols)] = tn(weight, out).astype(bf16)


def call(kernel, outs, *args, specs=None, scratch=(), flops=0):
    outs = [jax.ShapeDtypeStruct(*o) for o in outs]
    single = len(outs) == 1
    return pl.pallas_call(
        kernel,
        out_shape=outs[0] if single else outs,
        in_specs=specs or [VMEM] * len(args),
        out_specs=VMEM if single else [VMEM] * len(outs),
        scratch_shapes=scratch,
        cost_estimate=pl.CostEstimate(flops=flops, bytes_accessed=0, transcendentals=0) if flops else None,
        compiler_params=LIMIT,
    )(*args)


def far_off(*arrays):
    return [pltpu.with_memory_space_constraint(x, pltpu.HBM) for x in arrays]


def swap(x, *axes):
    if len(axes) == 1:
        return lax.ppermute(x, axes[0], [(0, 1), (1, 0)])
    return lax.ppermute(x, axes, [(i, 3 - i) for i in range(4)])


def turn(x, n, k):
    return lax.ppermute(x, "seq", [(i, (i + k) % n) for i in range(n)])


def later(x, n, k):
    return lax.ppermute(x, "seq", [(i, i + k) for i in range(n - k)])


def added(a, b):
    return (a.astype(f32) + b.astype(f32)).astype(bf16)


def after(x, *others):
    return lax.optimization_barrier((x, *others))[0]


def blockwise(queries, keys, values, resid, w_in, w_out, routes, gate_num):
    events, cols = queries.shape
    heads = cols // HD
    n = lax.axis_size("seq")
    capacity = 2 * TOP * events // (n * 2)
    s, m, r = lax.axis_index("seq"), lax.axis_index("mp"), lax.axis_index("rep")
    idx = jnp.stack(
        [s * 2 + r, m * 2 + r, m * 2 + 1 - r, (1 - m) * 2 + r, (1 - m) * 2 + 1 - r]
    ).astype(jnp.int32)
    wide, narrow = ((events, cols), f32), ((events, cols), bf16)
    buffer = [pltpu.VMEM((events, cols), bf16), pltpu.SemaphoreType.DMA((2,))]

    state, key, value = call(
        functools.partial(state_kernel, heads), [((heads * HD + 16, HD), bf16), narrow, narrow],
        *far_off(keys, values), specs=[HBM] * 2, scratch=buffer,
    )
    states = [later(state, n, k) for k in range(1, n)]
    num, den, query, resid_near = call(
        functools.partial(local_kernel, heads), [wide, wide, narrow, narrow],
        *far_off(queries, resid), key, value, specs=[HBM] * 2 + [VMEM] * 2, scratch=buffer,
    )
    table = jnp.concatenate([routes.T, gate_num.T], axis=0).astype(bf16)
    table = jnp.pad(table, ((0, 8 - 2 * TOP), (0, cols - events)))
    attended, squares = call(
        functools.partial(carry_kernel, heads), [wide, ((8, events), f32)],
        query, num, den, *states,
    )
    mixed, payload = call(
        mix_kernel, [narrow, ((events + 8, cols), bf16)], resid_near, attended, table,
        squares, swap(squares, "rep"), swap(squares, "mp"), swap(squares, "mp", "rep"),
    )

    weights = (w_in[0], w_out[0])
    hidden = w_in.shape[2]

    mine, table, across, beside, corner = {}, {}, {}, {}, {}
    arrived, send, keep, back, near, far, cross, part, home = {}, {}, {}, {}, {}, {}, {}, {}, {}

    def received(k, block):
        mine[k] = mixed if k == 0 else lax.slice_in_dim(block, 0, events)
        table[k] = lax.slice_in_dim(block, events, events + 8)
        across[k], beside[k] = swap(mine[k], "mp"), swap(mine[k], "rep")

    for k in (1, 2, 3):
        arrived[k] = turn(payload, n, k)
    received(0, payload)
    vals = {}
    def gate(x, step, k):
        deps = [vals[d] for d in WAITS.get((step, k), ())]
        return after(x, *deps) if deps else x
    for step, k in STEPS:
        if step == "z":
            last = gate(arrived[k], step, k)
            received(k, last)
        elif step == "x":
            across[k] = last = gate(across[k], step, k)
            corner[k] = swap(last, "rep")
        elif step == "k":
            keep[k], send[k] = call(
                functools.partial(expert_kernel, capacity), [((events, 2 * cols), bf16)] * 2,
                idx, table[k], mine[k], beside[k], across[k], gate(corner[k], step, k), *weights,
                specs=[SMEM] + [VMEM] * 7,
            )
            last = send[k]
            back[k] = swap(last, "rep")
        elif step == "f":
            both = keep[k].astype(f32) + gate(back[k], step, k).astype(f32)
            near[k], far[k] = both[:, :cols].astype(bf16), both[:, cols:].astype(bf16)
            last = far[k]
            cross[k] = swap(last, "mp")
        else:
            whole = near[k].astype(f32) + gate(cross[k], step, k).astype(f32)
            if k == 3:
                whole = whole + home.pop(2).astype(f32)
            part[k] = last = whole.astype(bf16)
            if k:
                home[k] = turn(last, n, (3 - k) % n if k == 2 else n - k)
        vals[(step, k)] = last
    total = mixed.astype(f32) + part[0].astype(f32)
    for x in home.values():
        total = total + x.astype(f32)
    return total.astype(bf16)


def shards(*args):
    blocky = lax.axis_size("mp") == 2 and lax.axis_size("rep") == 2 and lax.axis_size("seq") == 4
    return (blockwise if blocky else general)(*args)


def solution(mesh):
    in_specs = (
        P(("groups", "seq"), ("mp", "rep")),
        P(("groups", "seq"), ("mp", "rep")),
        P(("groups", "seq"), ("mp", "rep")),
        P(("groups", "seq"), ("mp", "rep")),
        P(("seq", "rep"), None, "mp"),
        P(("seq", "rep"), "mp", None),
        P(("groups", "seq"), None),
        P(("groups", "seq"), None),
    )
    out_specs = P(("groups", "seq"), ("mp", "rep"))
    return jax.shard_map(shards, mesh=mesh, in_specs=in_specs, out_specs=out_specs, check_vma=False)
```

```python
import functools

import jax
import jax.numpy as jnp
from jax import lax
from jax.experimental import pallas as pl
from jax.experimental.pallas import tpu as pltpu
from jax.sharding import PartitionSpec as P

D = 2048
HD = 128
TOP = 2

STEPS = (
    ("t", 1),
    ("z", 0),
    ("z", 1),
    ("t", 2),
    ("z", 2),
    ("t", 3),
    ("z", 3),
    ("a", 0),
    ("a", 2),
    ("d", 0),
    ("d", 1),
    ("d", 2),
    ("d", 3),
    ("b", 0),
    ("b", 1),
    ("b", 2),
    ("b", 3),
    ("x", 0),
    ("a", 1),
    ("x", 1),
    ("x", 2),
    ("a", 3),
    ("x", 3),
    ("k", 0),
    ("k", 1),
    ("k", 2),
    ("k", 3),
    ("f", 0),
    ("f", 2),
    ("n", 0),
    ("n", 1),
    ("n", 2),
    ("n", 3),
    ("p", 0),
    ("f", 1),
    ("p", 1),
    ("p", 2),
    ("f", 3),
    ("p", 3),
)
WAITS = {
    ("a", 1): (("x", 0),),
    ("a", 3): (("x", 2),),
    ("f", 0): (("x", 1),),
    ("f", 2): (("x", 3),),
    ("f", 1): (("p", 0),),
    ("f", 3): (("p", 2),),
}

RELAY, RETURN, SPLIT, WORK = 4, 3, True, 2000000000


gate_scale = 1.0 / 256.0
highest = lax.Precision.HIGHEST
f32 = jnp.float32
bf16 = jnp.bfloat16
VMEM = pl.BlockSpec(memory_space=pltpu.VMEM)
SMEM = pl.BlockSpec(memory_space=pltpu.SMEM)
HBM = pl.BlockSpec(memory_space=pltpu.HBM)
LIMIT = pltpu.CompilerParams(vmem_limit_bytes=24 * 1024 * 1024)


def feature(inputs_raw):
    wide = inputs_raw.astype(f32)
    return jnp.where(wide > 0.0, wide + 1.0, jnp.exp(jnp.minimum(wide, 0.0)))


def heads_first(matrix, head_width):
    return matrix.reshape(matrix.shape[0], -1, head_width).transpose(1, 0, 2)


def general(queries, keys, values, resid, w_in, w_out, routes, gate_num):
    tok_count, col_count = queries.shape
    seq_count = lax.axis_size("seq")
    rep_count = lax.axis_size("rep")
    expert_count = seq_count * rep_count
    capacity = 2 * TOP * tok_count // expert_count
    slot_count = expert_count * capacity
    query_feat = heads_first(feature(queries), HD)
    key_feat = heads_first(feature(keys), HD)
    value_heads = heads_first(values.astype(f32), HD)
    memory = jnp.einsum("hsc,hsd->hcd", key_feat, value_heads, precision=highest)
    key_total = jnp.sum(key_feat, axis=1)
    state = jnp.concatenate([memory, key_total[:, None, :]], axis=1).astype(bf16)
    states = lax.all_gather(state, "seq").astype(f32)
    earlier = jnp.arange(seq_count) < lax.axis_index("seq")
    state = jnp.sum(jnp.where(earlier[:, None, None, None], states, 0.0), axis=0)
    before, before_total = state[:, :HD], state[:, HD]
    causal = jnp.tril(jnp.ones((tok_count, tok_count), f32))
    scores = jnp.einsum("htc,hsc->hts", query_feat, key_feat, precision=highest) * causal
    numerator = jnp.einsum("hts,hsd->htd", scores, value_heads, precision=highest)
    numerator = numerator + jnp.einsum("htc,hcd->htd", query_feat, before, precision=highest)
    denominator = jnp.sum(scores, axis=-1) + jnp.einsum(
        "htc,hc->ht", query_feat, before_total, precision=highest
    )
    attended = numerator / denominator[..., None]
    local_squares = jnp.sum(attended * attended, axis=(0, 2))
    row_squares = lax.psum(local_squares, ("mp", "rep"))
    normed = attended * lax.rsqrt(row_squares / D + 1e-06)[None, :, None]
    mixed_rows = (
        resid.astype(f32) + normed.transpose(1, 0, 2).reshape(tok_count, col_count)
    ).astype(bf16)
    routed = routes.reshape(-1)
    onehot = (routed[:, None] == jnp.arange(expert_count, dtype=jnp.int32)[None, :]).astype(f32)
    pairs = jnp.arange(tok_count * TOP)
    below = (pairs[:, None] > pairs[None, :]).astype(f32)
    counts = jnp.dot(below, onehot, precision=highest)
    slot_rank = jnp.sum(counts * onehot, axis=1).astype(jnp.int32)
    slot_index = (routed // rep_count * capacity + slot_rank) * rep_count + routed % rep_count
    matches = (slot_index[:, None] == jnp.arange(slot_count, dtype=jnp.int32)[None, :]).astype(f32)
    matches = matches.reshape(tok_count, TOP, slot_count)
    picker = jnp.sum(matches, axis=1).astype(bf16)
    weights = gate_num.astype(f32) * gate_scale
    combine = jnp.einsum("tk,tks->ts", weights, matches, precision=highest)
    outgoing = jnp.einsum("ts,tc->sc", picker, mixed_rows, preferred_element_type=f32).astype(bf16)

    def exchange(rows):
        rows = rows.reshape(seq_count, capacity, rep_count, col_count)
        rows = lax.all_to_all(rows, "seq", split_axis=0, concat_axis=0, tiled=True)
        return lax.all_to_all(rows, "rep", split_axis=2, concat_axis=2, tiled=True)

    expert_rows = exchange(outgoing).reshape(seq_count * capacity, rep_count * col_count)
    preact = jnp.dot(
        lax.all_gather(expert_rows, "mp", axis=1, tiled=True), w_in[0], preferred_element_type=f32
    )
    hidden = jax.nn.gelu(preact).astype(bf16)
    partial_value = jnp.dot(hidden, w_out[0], preferred_element_type=f32)
    summed = lax.psum_scatter(partial_value.astype(bf16), "mp", scatter_dimension=1, tiled=True)
    returned = exchange(summed).astype(f32)
    expert_mix = jnp.dot(combine, returned.reshape(slot_count, col_count), precision=highest)
    return (mixed_rows.astype(f32) + expert_mix).astype(bf16)


def nt(a, b):
    return lax.dot_general(a, b, (((1,), (1,)), ((), ())), preferred_element_type=f32)


def tn(a, b):
    return lax.dot_general(a, b, (((0,), (0,)), ((), ())), preferred_element_type=f32)


def state_kernel(heads, k_hbm, v_hbm, state_ref, key_ref, v_ref, k_buf, sem):
    copy_k = pltpu.make_async_copy(k_hbm, k_buf, sem.at[0])
    copy_v = pltpu.make_async_copy(v_hbm, v_ref, sem.at[1])
    copy_k.start()
    copy_v.start()
    copy_k.wait()
    copy_v.wait()
    totals = []
    for h in range(heads):
        cols = pl.ds(h * HD, HD)
        key = feature(k_buf[:, cols])
        narrow = key.astype(bf16)
        key_ref[:, cols] = narrow
        state_ref[pl.ds(h * HD, HD), :] = tn(v_ref[:, cols], narrow).astype(bf16)
        totals.append(jnp.sum(key, axis=0, keepdims=True))
    totals.append(jnp.zeros((16 - heads, HD), f32))
    state_ref[pl.ds(heads * HD, 16), :] = jnp.concatenate(totals, axis=0).astype(bf16)


def local_kernel(heads, q_hbm, resid_hbm, key_ref, v_ref, num_ref, den_ref, query_ref, resid_ref, q_buf, sem):
    copy_q = pltpu.make_async_copy(q_hbm, q_buf, sem.at[0])
    copy_r = pltpu.make_async_copy(resid_hbm, resid_ref, sem.at[1])
    copy_q.start()
    copy_r.start()
    rows = q_buf.shape[0]
    t = lax.broadcasted_iota(jnp.int32, (rows, rows), 0)
    s = lax.broadcasted_iota(jnp.int32, (rows, rows), 1)
    copy_q.wait()
    for h in range(heads):
        cols = pl.ds(h * HD, HD)
        query = feature(q_buf[:, cols]).astype(bf16)
        query_ref[:, cols] = query
        scores = jnp.where(s <= t, nt(query, key_ref[:, cols]), 0.0).astype(bf16)
        num_ref[:, cols] = jnp.dot(scores, v_ref[:, cols], preferred_element_type=f32)
        den_ref[:, cols] = jnp.dot(scores, jnp.ones((rows, HD), bf16), preferred_element_type=f32)
    copy_r.wait()


def carry_kernel(heads, query_ref, num_ref, den_ref, *refs):
    states, (att_ref, sq_ref) = refs[:-2], refs[-2:]
    squares = jnp.zeros((query_ref.shape[0], HD), f32)
    carried = states[0][...].astype(f32)
    for extra in states[1:]:
        carried = carried + extra[...].astype(f32)
    carried = carried.astype(bf16)
    for h in range(heads):
        cols = pl.ds(h * HD, HD)
        query = query_ref[:, cols]
        top = num_ref[:, cols] + nt(query, carried[h * HD : (h + 1) * HD])
        total = jnp.broadcast_to(carried[heads * HD + h : heads * HD + h + 1], (HD, HD))
        attended = top / (den_ref[:, cols] + nt(query, total))
        att_ref[:, cols] = attended
        squares = squares + attended * attended
    sq_ref[...] = lax.dot_general(
        jnp.ones((8, HD), f32), squares, (((1,), (1,)), ((), ())),
        preferred_element_type=f32, precision=highest,
    )


def mix_kernel(resid_ref, att_ref, table_ref, *refs):
    squares, (mixed_ref, payload_ref) = refs[:-2], refs[-2:]
    rows = mixed_ref.shape[0]
    total = squares[0][...]
    for extra in squares[1:]:
        total = total + extra[...]
    column = jnp.transpose(lax.rsqrt(total * (1.0 / D) + 1e-06))[:, :1]
    mixed = (resid_ref[...].astype(f32) + att_ref[...] * column).astype(bf16)
    mixed_ref[...] = mixed
    payload_ref[pl.ds(0, rows), :] = mixed
    payload_ref[pl.ds(rows, 8), :] = table_ref[...]


def expert_kernel(capacity, idx_ref, table_ref, t0, t1, t2, t3, w_in_ref, w_out_ref, keep_ref, send_ref):
    events, cols = t0.shape
    at = [pl.ds(pl.multiple_of(idx_ref[1 + j] * cols, cols), cols) for j in range(4)]
    table = table_ref[...].astype(f32)[:, :events]
    expert = idx_ref[0].astype(f32)
    first, second = table[0:1] == expert, table[1:2] == expert
    named = first | second
    gate = jnp.where(first, table[2:3], table[3:4]) * gate_scale
    a = lax.broadcasted_iota(jnp.int32, (events, events), 0)
    b = lax.broadcasted_iota(jnp.int32, (events, events), 1)
    flag = jnp.broadcast_to(jnp.where(named, 1.0, 0.0), (8, events)).astype(bf16)
    rank = jnp.dot(flag, jnp.where(a < b, 1.0, 0.0).astype(bf16), preferred_element_type=f32)
    slot = jnp.where(named, rank[0:1], -1.0)
    hit = lax.broadcasted_iota(jnp.int32, (capacity, events), 0).astype(f32) == slot
    pick = jnp.where(hit, 1.0, 0.0).astype(bf16)
    weight = jnp.where(hit, gate, 0.0).astype(bf16)
    acc = jnp.zeros((capacity, w_in_ref.shape[1]), f32)
    for j, t in enumerate((t0, t1, t2, t3)):
        rows = jnp.dot(pick, t[...], preferred_element_type=f32).astype(bf16)
        acc = acc + jnp.dot(rows, w_in_ref[at[j], :], preferred_element_type=f32)
    hidden = jax.nn.gelu(acc).astype(bf16)
    for j, (ref, half) in enumerate(((keep_ref, 0), (send_ref, 0), (keep_ref, 1), (send_ref, 1))):
        out = jnp.dot(hidden, w_out_ref[:, at[j]], preferred_element_type=f32).astype(bf16)
        ref[:, pl.ds(half * cols, cols)] = tn(weight, out).astype(bf16)


def call(kernel, outs, *args, specs=None, scratch=(), flops=0):
    outs = [jax.ShapeDtypeStruct(*o) for o in outs]
    single = len(outs) == 1
    return pl.pallas_call(
        kernel,
        out_shape=outs[0] if single else outs,
        in_specs=specs or [VMEM] * len(args),
        out_specs=VMEM if single else [VMEM] * len(outs),
        scratch_shapes=scratch,
        cost_estimate=pl.CostEstimate(flops=flops, bytes_accessed=0, transcendentals=0) if flops else None,
        compiler_params=LIMIT,
    )(*args)


def far_off(*arrays):
    return [pltpu.with_memory_space_constraint(x, pltpu.HBM) for x in arrays]


def swap(x, *axes):
    if len(axes) == 1:
        return lax.ppermute(x, axes[0], [(0, 1), (1, 0)])
    return lax.ppermute(x, axes, [(i, 3 - i) for i in range(4)])


def turn(x, n, k):
    return lax.ppermute(x, "seq", [(i, (i + k) % n) for i in range(n)])


def later(x, n, k):
    return lax.ppermute(x, "seq", [(i, i + k) for i in range(n - k)])


def added(a, b):
    return (a.astype(f32) + b.astype(f32)).astype(bf16)


def after(x, *others):
    return lax.optimization_barrier((x, *others))[0]


def blockwise(queries, keys, values, resid, w_in, w_out, routes, gate_num):
    events, cols = queries.shape
    heads = cols // HD
    n = lax.axis_size("seq")
    capacity = 2 * TOP * events // (n * 2)
    s, m, r = lax.axis_index("seq"), lax.axis_index("mp"), lax.axis_index("rep")
    idx = jnp.stack(
        [s * 2 + r, m * 2 + r, m * 2 + 1 - r, (1 - m) * 2 + r, (1 - m) * 2 + 1 - r]
    ).astype(jnp.int32)
    wide, narrow = ((events, cols), f32), ((events, cols), bf16)
    buffer = [pltpu.VMEM((events, cols), bf16), pltpu.SemaphoreType.DMA((2,))]

    state, key, value = call(
        functools.partial(state_kernel, heads), [((heads * HD + 16, HD), bf16), narrow, narrow],
        *far_off(keys, values), specs=[HBM] * 2, scratch=buffer,
    )
    states = [later(state, n, k) for k in range(1, n)]
    num, den, query, resid_near = call(
        functools.partial(local_kernel, heads), [wide, wide, narrow, narrow],
        *far_off(queries, resid), key, value, specs=[HBM] * 2 + [VMEM] * 2, scratch=buffer,
    )
    table = jnp.concatenate([routes.T, gate_num.T], axis=0).astype(bf16)
    table = jnp.pad(table, ((0, 8 - 2 * TOP), (0, cols - events)))
    attended, squares = call(
        functools.partial(carry_kernel, heads), [wide, ((8, events), f32)],
        query, num, den, *states,
    )
    mixed, payload = call(
        mix_kernel, [narrow, ((events + 8, cols), bf16)], resid_near, attended, table,
        squares, swap(squares, "rep"), swap(squares, "mp"), swap(squares, "mp", "rep"),
    )

    weights = (w_in[0], w_out[0])
    hidden = w_in.shape[2]

    mine, table, across, beside, corner = {}, {}, {}, {}, {}
    arrived, send, keep, back, near, far, cross, part, home = {}, {}, {}, {}, {}, {}, {}, {}, {}
    vals = {}

    def gate(x, step, k):
        deps = [vals[d] for d in WAITS.get((step, k), ())]
        return after(x, *deps) if deps else x

    def left(x):
        return x[:, :cols]

    def right(x):
        return x[:, cols:]

    for step, k in STEPS:
        if step == "t":
            if k == 2 and RELAY in (1, 3):
                arrived[k] = turn(gate(vals["z", RELAY], step, k), n, (2 - RELAY) % n)
            elif k > 1 and RELAY == 4:
                arrived[k] = turn(gate(vals["z", k - 1], step, k), n, 1)
            else:
                arrived[k] = turn(gate(payload, step, k), n, k)
            continue
        elif step == "z":
            last = gate(arrived[k], step, k) if k else payload
            table[k] = lax.slice_in_dim(last, events, events + 8)
            mine[k] = lax.slice_in_dim(last, 0, events) if k else mixed
        elif step == "a":
            across[k] = swap(gate(mine[k], step, k), "mp")
            continue
        elif step == "d":
            beside[k] = swap(gate(mine[k], step, k), "rep")
            continue
        elif step == "b":
            beside[k] = last = gate(beside[k], step, k)
        elif step == "x":
            across[k] = last = gate(across[k], step, k)
            corner[k] = swap(last, "rep")
        elif step == "k":
            keep[k], send[k] = call(
                functools.partial(expert_kernel, capacity), [((events, 2 * cols), bf16)] * 2,
                idx, table[k], mine[k], beside[k], across[k], gate(corner[k], step, k), *weights,
                specs=[SMEM] + [VMEM] * 7,
                flops=WORK,
            )
            last = send[k]
            if SPLIT:
                back[k] = swap(right(last), "rep")
            else:
                back[k] = swap(last, "rep")
        elif step == "f":
            got = gate(back[k], step, k)
            if SPLIT:
                last = added(right(keep[k]), got)
            else:
                both = added(keep[k], got)
                near[k], last = left(both), right(both)
            cross[k] = swap(last, "mp")
        elif step == "n":
            if SPLIT:
                near[k] = swap(gate(left(send[k]), step, k), "rep")
            continue
        else:
            got = gate(cross[k], step, k)
            whole = near[k].astype(f32) + got.astype(f32)
            if SPLIT:
                whole = whole + left(keep[k]).astype(f32)
            if RETURN and k == RETURN and k < 4:
                whole = whole + home.pop(2).astype(f32)
            if RETURN == 4 and k > 1:
                whole = whole + home.pop(k - 1).astype(f32)
            part[k] = last = whole.astype(bf16)
            if k and RETURN == 4:
                home[k] = turn(last, n, 1)
            elif k:
                home[k] = turn(last, n, (RETURN - k) % n if RETURN and k == 2 else n - k)
        vals[step, k] = last
    total = mixed.astype(f32) + part[0].astype(f32)
    for x in home.values():
        total = total + x.astype(f32)
    return total.astype(bf16)


def shards(*args):
    blocky = lax.axis_size("mp") == 2 and lax.axis_size("rep") == 2 and lax.axis_size("seq") == 4
    return (blockwise if blocky else general)(*args)


def solution(mesh):
    in_specs = (
        P(("groups", "seq"), ("mp", "rep")),
        P(("groups", "seq"), ("mp", "rep")),
        P(("groups", "seq"), ("mp", "rep")),
        P(("groups", "seq"), ("mp", "rep")),
        P(("seq", "rep"), None, "mp"),
        P(("seq", "rep"), "mp", None),
        P(("groups", "seq"), None),
        P(("groups", "seq"), None),
    )
    out_specs = P(("groups", "seq"), ("mp", "rep"))
    return jax.shard_map(shards, mesh=mesh, in_specs=in_specs, out_specs=out_specs, check_vma=False)
```

```python
import functools

import jax
import jax.numpy as jnp
from jax import lax
from jax.experimental import pallas as pl
from jax.experimental.pallas import tpu as pltpu
from jax.sharding import PartitionSpec as P

D = 2048
HD = 128
TOP = 2

STEPS = (
    ("t", 1),
    ("z", 0),
    ("z", 1),
    ("t", 2),
    ("z", 2),
    ("t", 3),
    ("z", 3),
    ("a", 0),
    ("a", 1),
    ("a", 2),
    ("d", 0),
    ("d", 1),
    ("d", 2),
    ("d", 3),
    ("b", 0),
    ("b", 1),
    ("b", 2),
    ("b", 3),
    ("x", 0),
    ("x", 1),
    ("x", 2),
    ("a", 3),
    ("x", 3),
    ("k", 0),
    ("k", 1),
    ("k", 2),
    ("k", 3),
    ("f", 0),
    ("f", 2),
    ("n", 0),
    ("n", 1),
    ("n", 2),
    ("n", 3),
    ("p", 0),
    ("f", 1),
    ("p", 1),
    ("p", 2),
    ("f", 3),
    ("p", 3),
)
WAITS = {
    ("a", 3): (("x", 2),),
    ("f", 0): (("x", 1),),
    ("f", 2): (("x", 3),),
    ("f", 1): (("p", 0),),
    ("f", 3): (("p", 2),),
}

RELAY, RETURN, SPLIT, WORK = 4, 3, True, 2000000000


gate_scale = 1.0 / 256.0
highest = lax.Precision.HIGHEST
f32 = jnp.float32
bf16 = jnp.bfloat16
VMEM = pl.BlockSpec(memory_space=pltpu.VMEM)
SMEM = pl.BlockSpec(memory_space=pltpu.SMEM)
HBM = pl.BlockSpec(memory_space=pltpu.HBM)
LIMIT = pltpu.CompilerParams(vmem_limit_bytes=24 * 1024 * 1024)


def feature(inputs_raw):
    wide = inputs_raw.astype(f32)
    return jnp.where(wide > 0.0, wide + 1.0, jnp.exp(jnp.minimum(wide, 0.0)))


def heads_first(matrix, head_width):
    return matrix.reshape(matrix.shape[0], -1, head_width).transpose(1, 0, 2)


def general(queries, keys, values, resid, w_in, w_out, routes, gate_num):
    tok_count, col_count = queries.shape
    seq_count = lax.axis_size("seq")
    rep_count = lax.axis_size("rep")
    expert_count = seq_count * rep_count
    capacity = 2 * TOP * tok_count // expert_count
    slot_count = expert_count * capacity
    query_feat = heads_first(feature(queries), HD)
    key_feat = heads_first(feature(keys), HD)
    value_heads = heads_first(values.astype(f32), HD)
    memory = jnp.einsum("hsc,hsd->hcd", key_feat, value_heads, precision=highest)
    key_total = jnp.sum(key_feat, axis=1)
    state = jnp.concatenate([memory, key_total[:, None, :]], axis=1).astype(bf16)
    states = lax.all_gather(state, "seq").astype(f32)
    earlier = jnp.arange(seq_count) < lax.axis_index("seq")
    state = jnp.sum(jnp.where(earlier[:, None, None, None], states, 0.0), axis=0)
    before, before_total = state[:, :HD], state[:, HD]
    causal = jnp.tril(jnp.ones((tok_count, tok_count), f32))
    scores = jnp.einsum("htc,hsc->hts", query_feat, key_feat, precision=highest) * causal
    numerator = jnp.einsum("hts,hsd->htd", scores, value_heads, precision=highest)
    numerator = numerator + jnp.einsum("htc,hcd->htd", query_feat, before, precision=highest)
    denominator = jnp.sum(scores, axis=-1) + jnp.einsum(
        "htc,hc->ht", query_feat, before_total, precision=highest
    )
    attended = numerator / denominator[..., None]
    local_squares = jnp.sum(attended * attended, axis=(0, 2))
    row_squares = lax.psum(local_squares, ("mp", "rep"))
    normed = attended * lax.rsqrt(row_squares / D + 1e-06)[None, :, None]
    mixed_rows = (
        resid.astype(f32) + normed.transpose(1, 0, 2).reshape(tok_count, col_count)
    ).astype(bf16)
    routed = routes.reshape(-1)
    onehot = (routed[:, None] == jnp.arange(expert_count, dtype=jnp.int32)[None, :]).astype(f32)
    pairs = jnp.arange(tok_count * TOP)
    below = (pairs[:, None] > pairs[None, :]).astype(f32)
    counts = jnp.dot(below, onehot, precision=highest)
    slot_rank = jnp.sum(counts * onehot, axis=1).astype(jnp.int32)
    slot_index = (routed // rep_count * capacity + slot_rank) * rep_count + routed % rep_count
    matches = (slot_index[:, None] == jnp.arange(slot_count, dtype=jnp.int32)[None, :]).astype(f32)
    matches = matches.reshape(tok_count, TOP, slot_count)
    picker = jnp.sum(matches, axis=1).astype(bf16)
    weights = gate_num.astype(f32) * gate_scale
    combine = jnp.einsum("tk,tks->ts", weights, matches, precision=highest)
    outgoing = jnp.einsum("ts,tc->sc", picker, mixed_rows, preferred_element_type=f32).astype(bf16)

    def exchange(rows):
        rows = rows.reshape(seq_count, capacity, rep_count, col_count)
        rows = lax.all_to_all(rows, "seq", split_axis=0, concat_axis=0, tiled=True)
        return lax.all_to_all(rows, "rep", split_axis=2, concat_axis=2, tiled=True)

    expert_rows = exchange(outgoing).reshape(seq_count * capacity, rep_count * col_count)
    preact = jnp.dot(
        lax.all_gather(expert_rows, "mp", axis=1, tiled=True), w_in[0], preferred_element_type=f32
    )
    hidden = jax.nn.gelu(preact).astype(bf16)
    partial_value = jnp.dot(hidden, w_out[0], preferred_element_type=f32)
    summed = lax.psum_scatter(partial_value.astype(bf16), "mp", scatter_dimension=1, tiled=True)
    returned = exchange(summed).astype(f32)
    expert_mix = jnp.dot(combine, returned.reshape(slot_count, col_count), precision=highest)
    return (mixed_rows.astype(f32) + expert_mix).astype(bf16)


def nt(a, b):
    return lax.dot_general(a, b, (((1,), (1,)), ((), ())), preferred_element_type=f32)


def tn(a, b):
    return lax.dot_general(a, b, (((0,), (0,)), ((), ())), preferred_element_type=f32)


def state_kernel(heads, k_hbm, v_hbm, state_ref, key_ref, v_ref, k_buf, sem):
    copy_k = pltpu.make_async_copy(k_hbm, k_buf, sem.at[0])
    copy_v = pltpu.make_async_copy(v_hbm, v_ref, sem.at[1])
    copy_k.start()
    copy_v.start()
    copy_k.wait()
    copy_v.wait()
    totals = []
    for h in range(heads):
        cols = pl.ds(h * HD, HD)
        key = feature(k_buf[:, cols])
        narrow = key.astype(bf16)
        key_ref[:, cols] = narrow
        state_ref[pl.ds(h * HD, HD), :] = tn(v_ref[:, cols], narrow).astype(bf16)
        totals.append(jnp.sum(key, axis=0, keepdims=True))
    totals.append(jnp.zeros((16 - heads, HD), f32))
    state_ref[pl.ds(heads * HD, 16), :] = jnp.concatenate(totals, axis=0).astype(bf16)


def local_kernel(heads, q_hbm, resid_hbm, key_ref, v_ref, num_ref, den_ref, query_ref, resid_ref, q_buf, sem):
    copy_q = pltpu.make_async_copy(q_hbm, q_buf, sem.at[0])
    copy_r = pltpu.make_async_copy(resid_hbm, resid_ref, sem.at[1])
    copy_q.start()
    copy_r.start()
    rows = q_buf.shape[0]
    t = lax.broadcasted_iota(jnp.int32, (rows, rows), 0)
    s = lax.broadcasted_iota(jnp.int32, (rows, rows), 1)
    copy_q.wait()
    for h in range(heads):
        cols = pl.ds(h * HD, HD)
        query = feature(q_buf[:, cols]).astype(bf16)
        query_ref[:, cols] = query
        scores = jnp.where(s <= t, nt(query, key_ref[:, cols]), 0.0).astype(bf16)
        num_ref[:, cols] = jnp.dot(scores, v_ref[:, cols], preferred_element_type=f32)
        den_ref[:, cols] = jnp.dot(scores, jnp.ones((rows, HD), bf16), preferred_element_type=f32)
    copy_r.wait()


def carry_kernel(heads, query_ref, num_ref, den_ref, *refs):
    states, (att_ref, sq_ref) = refs[:-2], refs[-2:]
    squares = jnp.zeros((query_ref.shape[0], HD), f32)
    carried = states[0][...].astype(f32)
    for extra in states[1:]:
        carried = carried + extra[...].astype(f32)
    carried = carried.astype(bf16)
    for h in range(heads):
        cols = pl.ds(h * HD, HD)
        query = query_ref[:, cols]
        top = num_ref[:, cols] + nt(query, carried[h * HD : (h + 1) * HD])
        total = jnp.broadcast_to(carried[heads * HD + h : heads * HD + h + 1], (HD, HD))
        attended = top / (den_ref[:, cols] + nt(query, total))
        att_ref[:, cols] = attended
        squares = squares + attended * attended
    sq_ref[...] = lax.dot_general(
        jnp.ones((8, HD), f32), squares, (((1,), (1,)), ((), ())),
        preferred_element_type=f32, precision=highest,
    )


def mix_kernel(resid_ref, att_ref, table_ref, *refs):
    squares, (mixed_ref, payload_ref) = refs[:-2], refs[-2:]
    rows = mixed_ref.shape[0]
    total = squares[0][...]
    for extra in squares[1:]:
        total = total + extra[...]
    column = jnp.transpose(lax.rsqrt(total * (1.0 / D) + 1e-06))[:, :1]
    mixed = (resid_ref[...].astype(f32) + att_ref[...] * column).astype(bf16)
    mixed_ref[...] = mixed
    payload_ref[pl.ds(0, rows), :] = mixed
    payload_ref[pl.ds(rows, 8), :] = table_ref[...]


def expert_kernel(capacity, idx_ref, table_ref, t0, t1, t2, t3, w_in_ref, w_out_ref, keep_ref, send_ref):
    events, cols = t0.shape
    at = [pl.ds(pl.multiple_of(idx_ref[1 + j] * cols, cols), cols) for j in range(4)]
    table = table_ref[...].astype(f32)[:, :events]
    expert = idx_ref[0].astype(f32)
    first, second = table[0:1] == expert, table[1:2] == expert
    named = first | second
    gate = jnp.where(first, table[2:3], table[3:4]) * gate_scale
    a = lax.broadcasted_iota(jnp.int32, (events, events), 0)
    b = lax.broadcasted_iota(jnp.int32, (events, events), 1)
    flag = jnp.broadcast_to(jnp.where(named, 1.0, 0.0), (8, events)).astype(bf16)
    rank = jnp.dot(flag, jnp.where(a < b, 1.0, 0.0).astype(bf16), preferred_element_type=f32)
    slot = jnp.where(named, rank[0:1], -1.0)
    hit = lax.broadcasted_iota(jnp.int32, (capacity, events), 0).astype(f32) == slot
    pick = jnp.where(hit, 1.0, 0.0).astype(bf16)
    weight = jnp.where(hit, gate, 0.0).astype(bf16)
    acc = jnp.zeros((capacity, w_in_ref.shape[1]), f32)
    for j, t in enumerate((t0, t1, t2, t3)):
        rows = jnp.dot(pick, t[...], preferred_element_type=f32).astype(bf16)
        acc = acc + jnp.dot(rows, w_in_ref[at[j], :], preferred_element_type=f32)
    hidden = jax.nn.gelu(acc).astype(bf16)
    for j, (ref, half) in enumerate(((keep_ref, 0), (send_ref, 0), (keep_ref, 1), (send_ref, 1))):
        out = jnp.dot(hidden, w_out_ref[:, at[j]], preferred_element_type=f32).astype(bf16)
        ref[:, pl.ds(half * cols, cols)] = tn(weight, out).astype(bf16)


def call(kernel, outs, *args, specs=None, scratch=(), flops=0):
    outs = [jax.ShapeDtypeStruct(*o) for o in outs]
    single = len(outs) == 1
    return pl.pallas_call(
        kernel,
        out_shape=outs[0] if single else outs,
        in_specs=specs or [VMEM] * len(args),
        out_specs=VMEM if single else [VMEM] * len(outs),
        scratch_shapes=scratch,
        cost_estimate=pl.CostEstimate(flops=flops, bytes_accessed=0, transcendentals=0) if flops else None,
        compiler_params=LIMIT,
    )(*args)


def far_off(*arrays):
    return [pltpu.with_memory_space_constraint(x, pltpu.HBM) for x in arrays]


def swap(x, *axes):
    if len(axes) == 1:
        return lax.ppermute(x, axes[0], [(0, 1), (1, 0)])
    return lax.ppermute(x, axes, [(i, 3 - i) for i in range(4)])


def turn(x, n, k):
    return lax.ppermute(x, "seq", [(i, (i + k) % n) for i in range(n)])


def later(x, n, k):
    return lax.ppermute(x, "seq", [(i, i + k) for i in range(n - k)])


def added(a, b):
    return (a.astype(f32) + b.astype(f32)).astype(bf16)


def after(x, *others):
    return lax.optimization_barrier((x, *others))[0]


def blockwise(queries, keys, values, resid, w_in, w_out, routes, gate_num):
    events, cols = queries.shape
    heads = cols // HD
    n = lax.axis_size("seq")
    capacity = 2 * TOP * events // (n * 2)
    s, m, r = lax.axis_index("seq"), lax.axis_index("mp"), lax.axis_index("rep")
    idx = jnp.stack(
        [s * 2 + r, m * 2 + r, m * 2 + 1 - r, (1 - m) * 2 + r, (1 - m) * 2 + 1 - r]
    ).astype(jnp.int32)
    wide, narrow = ((events, cols), f32), ((events, cols), bf16)
    buffer = [pltpu.VMEM((events, cols), bf16), pltpu.SemaphoreType.DMA((2,))]

    state, key, value = call(
        functools.partial(state_kernel, heads), [((heads * HD + 16, HD), bf16), narrow, narrow],
        *far_off(keys, values), specs=[HBM] * 2, scratch=buffer,
    )
    states = [later(state, n, k) for k in range(1, n)]
    num, den, query, resid_near = call(
        functools.partial(local_kernel, heads), [wide, wide, narrow, narrow],
        *far_off(queries, resid), key, value, specs=[HBM] * 2 + [VMEM] * 2, scratch=buffer,
    )
    table = jnp.concatenate([routes.T, gate_num.T], axis=0).astype(bf16)
    table = jnp.pad(table, ((0, 8 - 2 * TOP), (0, cols - events)))
    attended, squares = call(
        functools.partial(carry_kernel, heads), [wide, ((8, events), f32)],
        query, num, den, *states,
    )
    mixed, payload = call(
        mix_kernel, [narrow, ((events + 8, cols), bf16)], resid_near, attended, table,
        squares, swap(squares, "rep"), swap(squares, "mp"), swap(squares, "mp", "rep"),
    )

    weights = (w_in[0], w_out[0])
    hidden = w_in.shape[2]

    mine, table, across, beside, corner = {}, {}, {}, {}, {}
    arrived, send, keep, back, near, far, cross, part, home = {}, {}, {}, {}, {}, {}, {}, {}, {}
    vals = {}

    def gate(x, step, k):
        deps = [vals[d] for d in WAITS.get((step, k), ())]
        return after(x, *deps) if deps else x

    def left(x):
        return x[:, :cols]

    def right(x):
        return x[:, cols:]

    for step, k in STEPS:
        if step == "t":
            if k == 2 and RELAY in (1, 3):
                arrived[k] = turn(gate(vals["z", RELAY], step, k), n, (2 - RELAY) % n)
            elif k > 1 and RELAY == 4:
                arrived[k] = turn(gate(vals["z", k - 1], step, k), n, 1)
            else:
                arrived[k] = turn(gate(payload, step, k), n, k)
            continue
        elif step == "z":
            last = gate(arrived[k], step, k) if k else payload
            table[k] = lax.slice_in_dim(last, events, events + 8)
            mine[k] = lax.slice_in_dim(last, 0, events) if k else mixed
        elif step == "a":
            across[k] = swap(gate(mine[k], step, k), "mp")
            continue
        elif step == "d":
            beside[k] = swap(gate(mine[k], step, k), "rep")
            continue
        elif step == "b":
            beside[k] = last = gate(beside[k], step, k)
        elif step == "x":
            across[k] = last = gate(across[k], step, k)
            corner[k] = swap(last, "rep")
        elif step == "k":
            keep[k], send[k] = call(
                functools.partial(expert_kernel, capacity), [((events, 2 * cols), bf16)] * 2,
                idx, table[k], mine[k], beside[k], across[k], gate(corner[k], step, k), *weights,
                specs=[SMEM] + [VMEM] * 7,
                flops=WORK,
            )
            last = send[k]
            if SPLIT:
                back[k] = swap(right(last), "rep")
            else:
                back[k] = swap(last, "rep")
        elif step == "f":
            got = gate(back[k], step, k)
            if SPLIT:
                last = added(right(keep[k]), got)
            else:
                both = added(keep[k], got)
                near[k], last = left(both), right(both)
            cross[k] = swap(last, "mp")
        elif step == "n":
            if SPLIT:
                near[k] = swap(gate(left(send[k]), step, k), "rep")
            continue
        else:
            got = gate(cross[k], step, k)
            whole = near[k].astype(f32) + got.astype(f32)
            if SPLIT:
                whole = whole + left(keep[k]).astype(f32)
            if RETURN and k == RETURN and k < 4:
                whole = whole + home.pop(2).astype(f32)
            if RETURN == 4 and k > 1:
                whole = whole + home.pop(k - 1).astype(f32)
            part[k] = last = whole.astype(bf16)
            if k and RETURN == 4:
                home[k] = turn(last, n, 1)
            elif k:
                home[k] = turn(last, n, (RETURN - k) % n if RETURN and k == 2 else n - k)
        vals[step, k] = last
    total = mixed.astype(f32) + part[0].astype(f32)
    for x in home.values():
        total = total + x.astype(f32)
    return total.astype(bf16)


def shards(*args):
    blocky = lax.axis_size("mp") == 2 and lax.axis_size("rep") == 2 and lax.axis_size("seq") == 4
    return (blockwise if blocky else general)(*args)


def solution(mesh):
    in_specs = (
        P(("groups", "seq"), ("mp", "rep")),
        P(("groups", "seq"), ("mp", "rep")),
        P(("groups", "seq"), ("mp", "rep")),
        P(("groups", "seq"), ("mp", "rep")),
        P(("seq", "rep"), None, "mp"),
        P(("seq", "rep"), "mp", None),
        P(("groups", "seq"), None),
        P(("groups", "seq"), None),
    )
    out_specs = P(("groups", "seq"), ("mp", "rep"))
    return jax.shard_map(shards, mesh=mesh, in_specs=in_specs, out_specs=out_specs, check_vma=False)
```

```python
import functools

import jax
import jax.numpy as jnp
from jax import lax
from jax.experimental import pallas as pl
from jax.experimental.pallas import tpu as pltpu
from jax.sharding import PartitionSpec as P

D = 2048
HD = 128
TOP = 2

STEPS = (
    ("t", 1),
    ("z", 0),
    ("z", 1),
    ("t", 2),
    ("z", 2),
    ("t", 3),
    ("z", 3),
    ("a", 0),
    ("a", 1),
    ("a", 2),
    ("a", 3),
    ("d", 0),
    ("d", 1),
    ("d", 2),
    ("d", 3),
    ("b", 0),
    ("b", 1),
    ("b", 2),
    ("b", 3),
    ("x", 0),
    ("x", 1),
    ("x", 2),
    ("x", 3),
    ("k", 0),
    ("k", 1),
    ("k", 2),
    ("k", 3),
    ("f", 0),
    ("f", 2),
    ("n", 0),
    ("n", 1),
    ("n", 2),
    ("n", 3),
    ("p", 0),
    ("f", 1),
    ("p", 1),
    ("p", 2),
    ("f", 3),
    ("p", 3),
)
WAITS = {
    ("f", 0): (("x", 1),),
    ("f", 2): (("x", 3),),
    ("f", 1): (("p", 0),),
    ("f", 3): (("p", 2),),
}

RELAY, RETURN, SPLIT, WORK = 4, 3, True, 2000000000


gate_scale = 1.0 / 256.0
highest = lax.Precision.HIGHEST
f32 = jnp.float32
bf16 = jnp.bfloat16
VMEM = pl.BlockSpec(memory_space=pltpu.VMEM)
SMEM = pl.BlockSpec(memory_space=pltpu.SMEM)
HBM = pl.BlockSpec(memory_space=pltpu.HBM)
LIMIT = pltpu.CompilerParams(vmem_limit_bytes=24 * 1024 * 1024)


def feature(inputs_raw):
    wide = inputs_raw.astype(f32)
    return jnp.where(wide > 0.0, wide + 1.0, jnp.exp(jnp.minimum(wide, 0.0)))


def heads_first(matrix, head_width):
    return matrix.reshape(matrix.shape[0], -1, head_width).transpose(1, 0, 2)


def general(queries, keys, values, resid, w_in, w_out, routes, gate_num):
    tok_count, col_count = queries.shape
    seq_count = lax.axis_size("seq")
    rep_count = lax.axis_size("rep")
    expert_count = seq_count * rep_count
    capacity = 2 * TOP * tok_count // expert_count
    slot_count = expert_count * capacity
    query_feat = heads_first(feature(queries), HD)
    key_feat = heads_first(feature(keys), HD)
    value_heads = heads_first(values.astype(f32), HD)
    memory = jnp.einsum("hsc,hsd->hcd", key_feat, value_heads, precision=highest)
    key_total = jnp.sum(key_feat, axis=1)
    state = jnp.concatenate([memory, key_total[:, None, :]], axis=1).astype(bf16)
    states = lax.all_gather(state, "seq").astype(f32)
    earlier = jnp.arange(seq_count) < lax.axis_index("seq")
    state = jnp.sum(jnp.where(earlier[:, None, None, None], states, 0.0), axis=0)
    before, before_total = state[:, :HD], state[:, HD]
    causal = jnp.tril(jnp.ones((tok_count, tok_count), f32))
    scores = jnp.einsum("htc,hsc->hts", query_feat, key_feat, precision=highest) * causal
    numerator = jnp.einsum("hts,hsd->htd", scores, value_heads, precision=highest)
    numerator = numerator + jnp.einsum("htc,hcd->htd", query_feat, before, precision=highest)
    denominator = jnp.sum(scores, axis=-1) + jnp.einsum(
        "htc,hc->ht", query_feat, before_total, precision=highest
    )
    attended = numerator / denominator[..., None]
    local_squares = jnp.sum(attended * attended, axis=(0, 2))
    row_squares = lax.psum(local_squares, ("mp", "rep"))
    normed = attended * lax.rsqrt(row_squares / D + 1e-06)[None, :, None]
    mixed_rows = (
        resid.astype(f32) + normed.transpose(1, 0, 2).reshape(tok_count, col_count)
    ).astype(bf16)
    routed = routes.reshape(-1)
    onehot = (routed[:, None] == jnp.arange(expert_count, dtype=jnp.int32)[None, :]).astype(f32)
    pairs = jnp.arange(tok_count * TOP)
    below = (pairs[:, None] > pairs[None, :]).astype(f32)
    counts = jnp.dot(below, onehot, precision=highest)
    slot_rank = jnp.sum(counts * onehot, axis=1).astype(jnp.int32)
    slot_index = (routed // rep_count * capacity + slot_rank) * rep_count + routed % rep_count
    matches = (slot_index[:, None] == jnp.arange(slot_count, dtype=jnp.int32)[None, :]).astype(f32)
    matches = matches.reshape(tok_count, TOP, slot_count)
    picker = jnp.sum(matches, axis=1).astype(bf16)
    weights = gate_num.astype(f32) * gate_scale
    combine = jnp.einsum("tk,tks->ts", weights, matches, precision=highest)
    outgoing = jnp.einsum("ts,tc->sc", picker, mixed_rows, preferred_element_type=f32).astype(bf16)

    def exchange(rows):
        rows = rows.reshape(seq_count, capacity, rep_count, col_count)
        rows = lax.all_to_all(rows, "seq", split_axis=0, concat_axis=0, tiled=True)
        return lax.all_to_all(rows, "rep", split_axis=2, concat_axis=2, tiled=True)

    expert_rows = exchange(outgoing).reshape(seq_count * capacity, rep_count * col_count)
    preact = jnp.dot(
        lax.all_gather(expert_rows, "mp", axis=1, tiled=True), w_in[0], preferred_element_type=f32
    )
    hidden = jax.nn.gelu(preact).astype(bf16)
    partial_value = jnp.dot(hidden, w_out[0], preferred_element_type=f32)
    summed = lax.psum_scatter(partial_value.astype(bf16), "mp", scatter_dimension=1, tiled=True)
    returned = exchange(summed).astype(f32)
    expert_mix = jnp.dot(combine, returned.reshape(slot_count, col_count), precision=highest)
    return (mixed_rows.astype(f32) + expert_mix).astype(bf16)


def nt(a, b):
    return lax.dot_general(a, b, (((1,), (1,)), ((), ())), preferred_element_type=f32)


def tn(a, b):
    return lax.dot_general(a, b, (((0,), (0,)), ((), ())), preferred_element_type=f32)


def state_kernel(heads, k_hbm, v_hbm, state_ref, key_ref, v_ref, k_buf, sem):
    copy_k = pltpu.make_async_copy(k_hbm, k_buf, sem.at[0])
    copy_v = pltpu.make_async_copy(v_hbm, v_ref, sem.at[1])
    copy_k.start()
    copy_v.start()
    copy_k.wait()
    copy_v.wait()
    totals = []
    for h in range(heads):
        cols = pl.ds(h * HD, HD)
        key = feature(k_buf[:, cols])
        narrow = key.astype(bf16)
        key_ref[:, cols] = narrow
        state_ref[pl.ds(h * HD, HD), :] = tn(v_ref[:, cols], narrow).astype(bf16)
        totals.append(jnp.sum(key, axis=0, keepdims=True))
    totals.append(jnp.zeros((16 - heads, HD), f32))
    state_ref[pl.ds(heads * HD, 16), :] = jnp.concatenate(totals, axis=0).astype(bf16)


def local_kernel(heads, q_hbm, resid_hbm, key_ref, v_ref, num_ref, den_ref, query_ref, resid_ref, q_buf, sem):
    copy_q = pltpu.make_async_copy(q_hbm, q_buf, sem.at[0])
    copy_r = pltpu.make_async_copy(resid_hbm, resid_ref, sem.at[1])
    copy_q.start()
    copy_r.start()
    rows = q_buf.shape[0]
    t = lax.broadcasted_iota(jnp.int32, (rows, rows), 0)
    s = lax.broadcasted_iota(jnp.int32, (rows, rows), 1)
    copy_q.wait()
    for h in range(heads):
        cols = pl.ds(h * HD, HD)
        query = feature(q_buf[:, cols]).astype(bf16)
        query_ref[:, cols] = query
        scores = jnp.where(s <= t, nt(query, key_ref[:, cols]), 0.0).astype(bf16)
        num_ref[:, cols] = jnp.dot(scores, v_ref[:, cols], preferred_element_type=f32)
        den_ref[:, cols] = jnp.dot(scores, jnp.ones((rows, HD), bf16), preferred_element_type=f32)
    copy_r.wait()


def carry_kernel(heads, query_ref, num_ref, den_ref, *refs):
    states, (att_ref, sq_ref) = refs[:-2], refs[-2:]
    squares = jnp.zeros((query_ref.shape[0], HD), f32)
    carried = states[0][...].astype(f32)
    for extra in states[1:]:
        carried = carried + extra[...].astype(f32)
    carried = carried.astype(bf16)
    for h in range(heads):
        cols = pl.ds(h * HD, HD)
        query = query_ref[:, cols]
        top = num_ref[:, cols] + nt(query, carried[h * HD : (h + 1) * HD])
        total = jnp.broadcast_to(carried[heads * HD + h : heads * HD + h + 1], (HD, HD))
        attended = top / (den_ref[:, cols] + nt(query, total))
        att_ref[:, cols] = attended
        squares = squares + attended * attended
    sq_ref[...] = lax.dot_general(
        jnp.ones((8, HD), f32), squares, (((1,), (1,)), ((), ())),
        preferred_element_type=f32, precision=highest,
    )


def mix_kernel(resid_ref, att_ref, table_ref, *refs):
    squares, (mixed_ref, payload_ref) = refs[:-2], refs[-2:]
    rows = mixed_ref.shape[0]
    total = squares[0][...]
    for extra in squares[1:]:
        total = total + extra[...]
    column = jnp.transpose(lax.rsqrt(total * (1.0 / D) + 1e-06))[:, :1]
    mixed = (resid_ref[...].astype(f32) + att_ref[...] * column).astype(bf16)
    mixed_ref[...] = mixed
    payload_ref[pl.ds(0, rows), :] = mixed
    payload_ref[pl.ds(rows, 8), :] = table_ref[...]


def expert_kernel(capacity, idx_ref, table_ref, t0, t1, t2, t3, w_in_ref, w_out_ref, keep_ref, send_ref):
    events, cols = t0.shape
    at = [pl.ds(pl.multiple_of(idx_ref[1 + j] * cols, cols), cols) for j in range(4)]
    table = table_ref[...].astype(f32)[:, :events]
    expert = idx_ref[0].astype(f32)
    first, second = table[0:1] == expert, table[1:2] == expert
    named = first | second
    gate = jnp.where(first, table[2:3], table[3:4]) * gate_scale
    a = lax.broadcasted_iota(jnp.int32, (events, events), 0)
    b = lax.broadcasted_iota(jnp.int32, (events, events), 1)
    flag = jnp.broadcast_to(jnp.where(named, 1.0, 0.0), (8, events)).astype(bf16)
    rank = jnp.dot(flag, jnp.where(a < b, 1.0, 0.0).astype(bf16), preferred_element_type=f32)
    slot = jnp.where(named, rank[0:1], -1.0)
    hit = lax.broadcasted_iota(jnp.int32, (capacity, events), 0).astype(f32) == slot
    pick = jnp.where(hit, 1.0, 0.0).astype(bf16)
    weight = jnp.where(hit, gate, 0.0).astype(bf16)
    acc = jnp.zeros((capacity, w_in_ref.shape[1]), f32)
    for j, t in enumerate((t0, t1, t2, t3)):
        rows = jnp.dot(pick, t[...], preferred_element_type=f32).astype(bf16)
        acc = acc + jnp.dot(rows, w_in_ref[at[j], :], preferred_element_type=f32)
    hidden = jax.nn.gelu(acc).astype(bf16)
    for j, (ref, half) in enumerate(((keep_ref, 0), (send_ref, 0), (keep_ref, 1), (send_ref, 1))):
        out = jnp.dot(hidden, w_out_ref[:, at[j]], preferred_element_type=f32).astype(bf16)
        ref[:, pl.ds(half * cols, cols)] = tn(weight, out).astype(bf16)


def call(kernel, outs, *args, specs=None, scratch=(), flops=0):
    outs = [jax.ShapeDtypeStruct(*o) for o in outs]
    single = len(outs) == 1
    return pl.pallas_call(
        kernel,
        out_shape=outs[0] if single else outs,
        in_specs=specs or [VMEM] * len(args),
        out_specs=VMEM if single else [VMEM] * len(outs),
        scratch_shapes=scratch,
        cost_estimate=pl.CostEstimate(flops=flops, bytes_accessed=0, transcendentals=0) if flops else None,
        compiler_params=LIMIT,
    )(*args)


def far_off(*arrays):
    return [pltpu.with_memory_space_constraint(x, pltpu.HBM) for x in arrays]


def swap(x, *axes):
    if len(axes) == 1:
        return lax.ppermute(x, axes[0], [(0, 1), (1, 0)])
    return lax.ppermute(x, axes, [(i, 3 - i) for i in range(4)])


def turn(x, n, k):
    return lax.ppermute(x, "seq", [(i, (i + k) % n) for i in range(n)])


def later(x, n, k):
    return lax.ppermute(x, "seq", [(i, i + k) for i in range(n - k)])


def added(a, b):
    return (a.astype(f32) + b.astype(f32)).astype(bf16)


def after(x, *others):
    return lax.optimization_barrier((x, *others))[0]


def blockwise(queries, keys, values, resid, w_in, w_out, routes, gate_num):
    events, cols = queries.shape
    heads = cols // HD
    n = lax.axis_size("seq")
    capacity = 2 * TOP * events // (n * 2)
    s, m, r = lax.axis_index("seq"), lax.axis_index("mp"), lax.axis_index("rep")
    idx = jnp.stack(
        [s * 2 + r, m * 2 + r, m * 2 + 1 - r, (1 - m) * 2 + r, (1 - m) * 2 + 1 - r]
    ).astype(jnp.int32)
    wide, narrow = ((events, cols), f32), ((events, cols), bf16)
    buffer = [pltpu.VMEM((events, cols), bf16), pltpu.SemaphoreType.DMA((2,))]

    state, key, value = call(
        functools.partial(state_kernel, heads), [((heads * HD + 16, HD), bf16), narrow, narrow],
        *far_off(keys, values), specs=[HBM] * 2, scratch=buffer,
    )
    states = [later(state, n, k) for k in range(1, n)]
    num, den, query, resid_near = call(
        functools.partial(local_kernel, heads), [wide, wide, narrow, narrow],
        *far_off(queries, resid), key, value, specs=[HBM] * 2 + [VMEM] * 2, scratch=buffer,
    )
    table = jnp.concatenate([routes.T, gate_num.T], axis=0).astype(bf16)
    table = jnp.pad(table, ((0, 8 - 2 * TOP), (0, cols - events)))
    attended, squares = call(
        functools.partial(carry_kernel, heads), [wide, ((8, events), f32)],
        query, num, den, *states,
    )
    mixed, payload = call(
        mix_kernel, [narrow, ((events + 8, cols), bf16)], resid_near, attended, table,
        squares, swap(squares, "rep"), swap(squares, "mp"), swap(squares, "mp", "rep"),
    )

    weights = (w_in[0], w_out[0])
    hidden = w_in.shape[2]

    mine, table, across, beside, corner = {}, {}, {}, {}, {}
    arrived, send, keep, back, near, far, cross, part, home = {}, {}, {}, {}, {}, {}, {}, {}, {}
    vals = {}

    def gate(x, step, k):
        deps = [vals[d] for d in WAITS.get((step, k), ())]
        return after(x, *deps) if deps else x

    def left(x):
        return x[:, :cols]

    def right(x):
        return x[:, cols:]

    for step, k in STEPS:
        if step == "t":
            if k == 2 and RELAY in (1, 3):
                arrived[k] = turn(gate(vals["z", RELAY], step, k), n, (2 - RELAY) % n)
            elif k > 1 and RELAY == 4:
                arrived[k] = turn(gate(vals["z", k - 1], step, k), n, 1)
            else:
                arrived[k] = turn(gate(payload, step, k), n, k)
            continue
        elif step == "z":
            last = gate(arrived[k], step, k) if k else payload
            table[k] = lax.slice_in_dim(last, events, events + 8)
            mine[k] = lax.slice_in_dim(last, 0, events) if k else mixed
        elif step == "a":
            across[k] = swap(gate(mine[k], step, k), "mp")
            continue
        elif step == "d":
            beside[k] = swap(gate(mine[k], step, k), "rep")
            continue
        elif step == "b":
            beside[k] = last = gate(beside[k], step, k)
        elif step == "x":
            across[k] = last = gate(across[k], step, k)
            corner[k] = swap(last, "rep")
        elif step == "k":
            keep[k], send[k] = call(
                functools.partial(expert_kernel, capacity), [((events, 2 * cols), bf16)] * 2,
                idx, table[k], mine[k], beside[k], across[k], gate(corner[k], step, k), *weights,
                specs=[SMEM] + [VMEM] * 7,
                flops=WORK,
            )
            last = send[k]
            if SPLIT:
                back[k] = swap(right(last), "rep")
            else:
                back[k] = swap(last, "rep")
        elif step == "f":
            got = gate(back[k], step, k)
            if SPLIT:
                last = added(right(keep[k]), got)
            else:
                both = added(keep[k], got)
                near[k], last = left(both), right(both)
            cross[k] = swap(last, "mp")
        elif step == "n":
            if SPLIT:
                near[k] = swap(gate(left(send[k]), step, k), "rep")
            continue
        else:
            got = gate(cross[k], step, k)
            whole = near[k].astype(f32) + got.astype(f32)
            if SPLIT:
                whole = whole + left(keep[k]).astype(f32)
            if RETURN and k == RETURN and k < 4:
                whole = whole + home.pop(2).astype(f32)
            if RETURN == 4 and k > 1:
                whole = whole + home.pop(k - 1).astype(f32)
            part[k] = last = whole.astype(bf16)
            if k and RETURN == 4:
                home[k] = turn(last, n, 1)
            elif k:
                home[k] = turn(last, n, (RETURN - k) % n if RETURN and k == 2 else n - k)
        vals[step, k] = last
    total = mixed.astype(f32) + part[0].astype(f32)
    for x in home.values():
        total = total + x.astype(f32)
    return total.astype(bf16)


def shards(*args):
    blocky = lax.axis_size("mp") == 2 and lax.axis_size("rep") == 2 and lax.axis_size("seq") == 4
    return (blockwise if blocky else general)(*args)


def solution(mesh):
    in_specs = (
        P(("groups", "seq"), ("mp", "rep")),
        P(("groups", "seq"), ("mp", "rep")),
        P(("groups", "seq"), ("mp", "rep")),
        P(("groups", "seq"), ("mp", "rep")),
        P(("seq", "rep"), None, "mp"),
        P(("seq", "rep"), "mp", None),
        P(("groups", "seq"), None),
        P(("groups", "seq"), None),
    )
    out_specs = P(("groups", "seq"), ("mp", "rep"))
    return jax.shard_map(shards, mesh=mesh, in_specs=in_specs, out_specs=out_specs, check_vma=False)
```

```python
import functools

import jax
import jax.numpy as jnp
from jax import lax
from jax.experimental import pallas as pl
from jax.experimental.pallas import tpu as pltpu
from jax.sharding import PartitionSpec as P

D = 2048
HD = 128
TOP = 2

STEPS = (
    ("t", 1),
    ("z", 0),
    ("z", 1),
    ("t", 2),
    ("z", 2),
    ("t", 3),
    ("z", 3),
    ("a", 0),
    ("a", 1),
    ("a", 2),
    ("d", 0),
    ("d", 1),
    ("d", 2),
    ("d", 3),
    ("b", 0),
    ("b", 1),
    ("b", 2),
    ("b", 3),
    ("x", 0),
    ("x", 1),
    ("x", 2),
    ("a", 3),
    ("x", 3),
    ("k", 0),
    ("k", 1),
    ("k", 2),
    ("k", 3),
    ("f", 0),
    ("f", 2),
    ("n", 0),
    ("n", 1),
    ("n", 2),
    ("n", 3),
    ("p", 0),
    ("f", 1),
    ("p", 1),
    ("p", 2),
    ("f", 3),
    ("p", 3),
)
WAITS = {
    ("a", 3): (("x", 2),),
    ("f", 0): (("x", 1),),
    ("f", 2): (("x", 3),),
    ("f", 1): (("p", 0),),
    ("f", 3): (("p", 2),),
}

RELAY, RETURN, SPLIT = 4, 3, True


gate_scale = 1.0 / 256.0
highest = lax.Precision.HIGHEST
f32 = jnp.float32
bf16 = jnp.bfloat16
VMEM = pl.BlockSpec(memory_space=pltpu.VMEM)
SMEM = pl.BlockSpec(memory_space=pltpu.SMEM)
HBM = pl.BlockSpec(memory_space=pltpu.HBM)
LIMIT = pltpu.CompilerParams(vmem_limit_bytes=24 * 1024 * 1024)


def feature(inputs_raw):
    wide = inputs_raw.astype(f32)
    return jnp.where(wide > 0.0, wide + 1.0, jnp.exp(jnp.minimum(wide, 0.0)))


def heads_first(matrix, head_width):
    return matrix.reshape(matrix.shape[0], -1, head_width).transpose(1, 0, 2)


def general(queries, keys, values, resid, w_in, w_out, routes, gate_num):
    tok_count, col_count = queries.shape
    seq_count = lax.axis_size("seq")
    rep_count = lax.axis_size("rep")
    expert_count = seq_count * rep_count
    capacity = 2 * TOP * tok_count // expert_count
    slot_count = expert_count * capacity
    query_feat = heads_first(feature(queries), HD)
    key_feat = heads_first(feature(keys), HD)
    value_heads = heads_first(values.astype(f32), HD)
    memory = jnp.einsum("hsc,hsd->hcd", key_feat, value_heads, precision=highest)
    key_total = jnp.sum(key_feat, axis=1)
    state = jnp.concatenate([memory, key_total[:, None, :]], axis=1).astype(bf16)
    states = lax.all_gather(state, "seq").astype(f32)
    earlier = jnp.arange(seq_count) < lax.axis_index("seq")
    state = jnp.sum(jnp.where(earlier[:, None, None, None], states, 0.0), axis=0)
    before, before_total = state[:, :HD], state[:, HD]
    causal = jnp.tril(jnp.ones((tok_count, tok_count), f32))
    scores = jnp.einsum("htc,hsc->hts", query_feat, key_feat, precision=highest) * causal
    numerator = jnp.einsum("hts,hsd->htd", scores, value_heads, precision=highest)
    numerator = numerator + jnp.einsum("htc,hcd->htd", query_feat, before, precision=highest)
    denominator = jnp.sum(scores, axis=-1) + jnp.einsum(
        "htc,hc->ht", query_feat, before_total, precision=highest
    )
    attended = numerator / denominator[..., None]
    local_squares = jnp.sum(attended * attended, axis=(0, 2))
    row_squares = lax.psum(local_squares, ("mp", "rep"))
    normed = attended * lax.rsqrt(row_squares / D + 1e-06)[None, :, None]
    mixed_rows = (
        resid.astype(f32) + normed.transpose(1, 0, 2).reshape(tok_count, col_count)
    ).astype(bf16)
    routed = routes.reshape(-1)
    onehot = (routed[:, None] == jnp.arange(expert_count, dtype=jnp.int32)[None, :]).astype(f32)
    pairs = jnp.arange(tok_count * TOP)
    below = (pairs[:, None] > pairs[None, :]).astype(f32)
    counts = jnp.dot(below, onehot, precision=highest)
    slot_rank = jnp.sum(counts * onehot, axis=1).astype(jnp.int32)
    slot_index = (routed // rep_count * capacity + slot_rank) * rep_count + routed % rep_count
    matches = (slot_index[:, None] == jnp.arange(slot_count, dtype=jnp.int32)[None, :]).astype(f32)
    matches = matches.reshape(tok_count, TOP, slot_count)
    picker = jnp.sum(matches, axis=1).astype(bf16)
    weights = gate_num.astype(f32) * gate_scale
    combine = jnp.einsum("tk,tks->ts", weights, matches, precision=highest)
    outgoing = jnp.einsum("ts,tc->sc", picker, mixed_rows, preferred_element_type=f32).astype(bf16)

    def exchange(rows):
        rows = rows.reshape(seq_count, capacity, rep_count, col_count)
        rows = lax.all_to_all(rows, "seq", split_axis=0, concat_axis=0, tiled=True)
        return lax.all_to_all(rows, "rep", split_axis=2, concat_axis=2, tiled=True)

    expert_rows = exchange(outgoing).reshape(seq_count * capacity, rep_count * col_count)
    preact = jnp.dot(
        lax.all_gather(expert_rows, "mp", axis=1, tiled=True), w_in[0], preferred_element_type=f32
    )
    hidden = jax.nn.gelu(preact).astype(bf16)
    partial_value = jnp.dot(hidden, w_out[0], preferred_element_type=f32)
    summed = lax.psum_scatter(partial_value.astype(bf16), "mp", scatter_dimension=1, tiled=True)
    returned = exchange(summed).astype(f32)
    expert_mix = jnp.dot(combine, returned.reshape(slot_count, col_count), precision=highest)
    return (mixed_rows.astype(f32) + expert_mix).astype(bf16)


def nt(a, b):
    return lax.dot_general(a, b, (((1,), (1,)), ((), ())), preferred_element_type=f32)


def tn(a, b):
    return lax.dot_general(a, b, (((0,), (0,)), ((), ())), preferred_element_type=f32)


def state_kernel(heads, k_hbm, v_hbm, state_ref, key_ref, v_ref, k_buf, sem):
    copy_k = pltpu.make_async_copy(k_hbm, k_buf, sem.at[0])
    copy_v = pltpu.make_async_copy(v_hbm, v_ref, sem.at[1])
    copy_k.start()
    copy_v.start()
    copy_k.wait()
    copy_v.wait()
    totals = []
    for h in range(heads):
        cols = pl.ds(h * HD, HD)
        key = feature(k_buf[:, cols])
        narrow = key.astype(bf16)
        key_ref[:, cols] = narrow
        state_ref[pl.ds(h * HD, HD), :] = tn(v_ref[:, cols], narrow).astype(bf16)
        totals.append(jnp.sum(key, axis=0, keepdims=True))
    totals.append(jnp.zeros((16 - heads, HD), f32))
    state_ref[pl.ds(heads * HD, 16), :] = jnp.concatenate(totals, axis=0).astype(bf16)


def local_kernel(heads, q_hbm, resid_hbm, key_ref, v_ref, num_ref, den_ref, query_ref, resid_ref, q_buf, sem):
    copy_q = pltpu.make_async_copy(q_hbm, q_buf, sem.at[0])
    copy_r = pltpu.make_async_copy(resid_hbm, resid_ref, sem.at[1])
    copy_q.start()
    copy_r.start()
    rows = q_buf.shape[0]
    t = lax.broadcasted_iota(jnp.int32, (rows, rows), 0)
    s = lax.broadcasted_iota(jnp.int32, (rows, rows), 1)
    copy_q.wait()
    for h in range(heads):
        cols = pl.ds(h * HD, HD)
        query = feature(q_buf[:, cols]).astype(bf16)
        query_ref[:, cols] = query
        scores = jnp.where(s <= t, nt(query, key_ref[:, cols]), 0.0).astype(bf16)
        num_ref[:, cols] = jnp.dot(scores, v_ref[:, cols], preferred_element_type=f32)
        den_ref[:, cols] = jnp.dot(scores, jnp.ones((rows, HD), bf16), preferred_element_type=f32)
    copy_r.wait()


def carry_kernel(heads, query_ref, num_ref, den_ref, *refs):
    states, (att_ref, sq_ref) = refs[:-2], refs[-2:]
    squares = jnp.zeros((query_ref.shape[0], HD), f32)
    carried = states[0][...].astype(f32)
    for extra in states[1:]:
        carried = carried + extra[...].astype(f32)
    carried = carried.astype(bf16)
    for h in range(heads):
        cols = pl.ds(h * HD, HD)
        query = query_ref[:, cols]
        top = num_ref[:, cols] + nt(query, carried[h * HD : (h + 1) * HD])
        total = jnp.broadcast_to(carried[heads * HD + h : heads * HD + h + 1], (HD, HD))
        attended = top / (den_ref[:, cols] + nt(query, total))
        att_ref[:, cols] = attended
        squares = squares + attended * attended
    sq_ref[...] = lax.dot_general(
        jnp.ones((8, HD), f32), squares, (((1,), (1,)), ((), ())),
        preferred_element_type=f32, precision=highest,
    )


def mix_kernel(resid_ref, att_ref, table_ref, *refs):
    squares, (mixed_ref, payload_ref) = refs[:-2], refs[-2:]
    rows = mixed_ref.shape[0]
    total = squares[0][...]
    for extra in squares[1:]:
        total = total + extra[...]
    column = jnp.transpose(lax.rsqrt(total * (1.0 / D) + 1e-06))[:, :1]
    mixed = (resid_ref[...].astype(f32) + att_ref[...] * column).astype(bf16)
    mixed_ref[...] = mixed
    payload_ref[pl.ds(0, rows), :] = mixed
    payload_ref[pl.ds(rows, 8), :] = table_ref[...]


def expert_kernel(capacity, idx_ref, table_ref, t0, t1, t2, t3, w_in_ref, w_out_ref, keep_ref, send_ref):
    events, cols = t0.shape
    at = [pl.ds(pl.multiple_of(idx_ref[1 + j] * cols, cols), cols) for j in range(4)]
    table = table_ref[...].astype(f32)[:, :events]
    expert = idx_ref[0].astype(f32)
    first, second = table[0:1] == expert, table[1:2] == expert
    named = first | second
    gate = jnp.where(first, table[2:3], table[3:4]) * gate_scale
    a = lax.broadcasted_iota(jnp.int32, (events, events), 0)
    b = lax.broadcasted_iota(jnp.int32, (events, events), 1)
    flag = jnp.broadcast_to(jnp.where(named, 1.0, 0.0), (8, events)).astype(bf16)
    rank = jnp.dot(flag, jnp.where(a < b, 1.0, 0.0).astype(bf16), preferred_element_type=f32)
    slot = jnp.where(named, rank[0:1], -1.0)
    hit = lax.broadcasted_iota(jnp.int32, (capacity, events), 0).astype(f32) == slot
    pick = jnp.where(hit, 1.0, 0.0).astype(bf16)
    weight = jnp.where(hit, gate, 0.0).astype(bf16)
    acc = jnp.zeros((capacity, w_in_ref.shape[1]), f32)
    for j, t in enumerate((t0, t1, t2, t3)):
        rows = jnp.dot(pick, t[...], preferred_element_type=f32).astype(bf16)
        acc = acc + jnp.dot(rows, w_in_ref[at[j], :], preferred_element_type=f32)
    hidden = jax.nn.gelu(acc).astype(bf16)
    for j, (ref, half) in enumerate(((keep_ref, 0), (send_ref, 0), (keep_ref, 1), (send_ref, 1))):
        out = jnp.dot(hidden, w_out_ref[:, at[j]], preferred_element_type=f32).astype(bf16)
        ref[:, pl.ds(half * cols, cols)] = tn(weight, out).astype(bf16)


def call(kernel, outs, *args, specs=None, scratch=(), flops=0):
    outs = [jax.ShapeDtypeStruct(*o) for o in outs]
    single = len(outs) == 1
    return pl.pallas_call(
        kernel,
        out_shape=outs[0] if single else outs,
        in_specs=specs or [VMEM] * len(args),
        out_specs=VMEM if single else [VMEM] * len(outs),
        scratch_shapes=scratch,
        cost_estimate=pl.CostEstimate(flops=flops, bytes_accessed=0, transcendentals=0) if flops else None,
        compiler_params=LIMIT,
    )(*args)


def far_off(*arrays):
    return [pltpu.with_memory_space_constraint(x, pltpu.HBM) for x in arrays]


def swap(x, *axes):
    if len(axes) == 1:
        return lax.ppermute(x, axes[0], [(0, 1), (1, 0)])
    return lax.ppermute(x, axes, [(i, 3 - i) for i in range(4)])


def turn(x, n, k):
    return lax.ppermute(x, "seq", [(i, (i + k) % n) for i in range(n)])


def later(x, n, k):
    return lax.ppermute(x, "seq", [(i, i + k) for i in range(n - k)])


def added(a, b):
    return (a.astype(f32) + b.astype(f32)).astype(bf16)


def after(x, *others):
    return lax.optimization_barrier((x, *others))[0]


def blockwise(queries, keys, values, resid, w_in, w_out, routes, gate_num):
    events, cols = queries.shape
    heads = cols // HD
    n = lax.axis_size("seq")
    capacity = 2 * TOP * events // (n * 2)
    s, m, r = lax.axis_index("seq"), lax.axis_index("mp"), lax.axis_index("rep")
    idx = jnp.stack(
        [s * 2 + r, m * 2 + r, m * 2 + 1 - r, (1 - m) * 2 + r, (1 - m) * 2 + 1 - r]
    ).astype(jnp.int32)
    wide, narrow = ((events, cols), f32), ((events, cols), bf16)
    buffer = [pltpu.VMEM((events, cols), bf16), pltpu.SemaphoreType.DMA((2,))]

    state, key, value = call(
        functools.partial(state_kernel, heads), [((heads * HD + 16, HD), bf16), narrow, narrow],
        *far_off(keys, values), specs=[HBM] * 2, scratch=buffer,
    )
    states = [later(state, n, k) for k in range(1, n)]
    num, den, query, resid_near = call(
        functools.partial(local_kernel, heads), [wide, wide, narrow, narrow],
        *far_off(queries, resid), key, value, specs=[HBM] * 2 + [VMEM] * 2, scratch=buffer,
    )
    table = jnp.concatenate([routes.T, gate_num.T], axis=0).astype(bf16)
    table = jnp.pad(table, ((0, 8 - 2 * TOP), (0, cols - events)))
    attended, squares = call(
        functools.partial(carry_kernel, heads), [wide, ((8, events), f32)],
        query, num, den, *states,
    )
    mixed, payload = call(
        mix_kernel, [narrow, ((events + 8, cols), bf16)], resid_near, attended, table,
        squares, swap(squares, "rep"), swap(squares, "mp"), swap(squares, "mp", "rep"),
    )

    weights = (w_in[0], w_out[0])
    hidden = w_in.shape[2]

    mine, table, across, beside, corner = {}, {}, {}, {}, {}
    arrived, send, keep, back, near, far, cross, part, home = {}, {}, {}, {}, {}, {}, {}, {}, {}
    vals = {}

    def gate(x, step, k):
        deps = [vals[d] for d in WAITS.get((step, k), ())]
        return after(x, *deps) if deps else x

    def left(x):
        return x[:, :cols]

    def right(x):
        return x[:, cols:]

    for step, k in STEPS:
        if step == "t":
            if k == 2 and RELAY in (1, 3):
                arrived[k] = turn(gate(vals["z", RELAY], step, k), n, (2 - RELAY) % n)
            elif k > 1 and RELAY == 4:
                arrived[k] = turn(gate(vals["z", k - 1], step, k), n, 1)
            else:
                arrived[k] = turn(gate(payload, step, k), n, k)
            continue
        elif step == "z":
            last = gate(arrived[k], step, k) if k else payload
            table[k] = lax.slice_in_dim(last, events, events + 8)
            mine[k] = lax.slice_in_dim(last, 0, events) if k else mixed
        elif step == "a":
            across[k] = swap(gate(mine[k], step, k), "mp")
            continue
        elif step == "d":
            beside[k] = swap(gate(mine[k], step, k), "rep")
            continue
        elif step == "b":
            beside[k] = last = gate(beside[k], step, k)
        elif step == "x":
            across[k] = last = gate(across[k], step, k)
            corner[k] = swap(last, "rep")
        elif step == "k":
            keep[k], send[k] = call(
                functools.partial(expert_kernel, capacity), [((events, 2 * cols), bf16)] * 2,
                idx, table[k], mine[k], beside[k], across[k], gate(corner[k], step, k), *weights,
                specs=[SMEM] + [VMEM] * 7,
                flops=16 * capacity * cols * (events + w_in.shape[2]),
            )
            last = send[k]
            if SPLIT:
                back[k] = swap(right(last), "rep")
            else:
                back[k] = swap(last, "rep")
        elif step == "f":
            got = gate(back[k], step, k)
            if SPLIT:
                last = added(right(keep[k]), got)
            else:
                both = added(keep[k], got)
                near[k], last = left(both), right(both)
            cross[k] = swap(last, "mp")
        elif step == "n":
            if SPLIT:
                near[k] = swap(gate(left(send[k]), step, k), "rep")
            continue
        else:
            got = gate(cross[k], step, k)
            whole = near[k].astype(f32) + got.astype(f32)
            if SPLIT:
                whole = whole + left(keep[k]).astype(f32)
            if RETURN and k == RETURN and k < 4:
                whole = whole + home.pop(2).astype(f32)
            if RETURN == 4 and k > 1:
                whole = whole + home.pop(k - 1).astype(f32)
            part[k] = last = whole.astype(bf16)
            if k and RETURN == 4:
                home[k] = turn(last, n, 1)
            elif k:
                home[k] = turn(last, n, (RETURN - k) % n if RETURN and k == 2 else n - k)
        vals[step, k] = last
    total = mixed.astype(f32) + part[0].astype(f32)
    for x in home.values():
        total = total + x.astype(f32)
    return total.astype(bf16)


def shards(*args):
    blocky = lax.axis_size("mp") == 2 and lax.axis_size("rep") == 2 and lax.axis_size("seq") == 4
    return (blockwise if blocky else general)(*args)


def solution(mesh):
    in_specs = (
        P(("groups", "seq"), ("mp", "rep")),
        P(("groups", "seq"), ("mp", "rep")),
        P(("groups", "seq"), ("mp", "rep")),
        P(("groups", "seq"), ("mp", "rep")),
        P(("seq", "rep"), None, "mp"),
        P(("seq", "rep"), "mp", None),
        P(("groups", "seq"), None),
        P(("groups", "seq"), None),
    )
    out_specs = P(("groups", "seq"), ("mp", "rep"))
    return jax.shard_map(shards, mesh=mesh, in_specs=in_specs, out_specs=out_specs, check_vma=False)
```
